256 devices in a mesh: stn: 16 (over x, y_lo, core), chan: 16 (over z, y_hi).
Axes of the slice: x: 4, y: 4 (y_hi: 2, y_lo: 2; y = y_hi * 2 + y_lo), z: 8, core: 2. Of those that a mesh axis runs over, the one named last changes fastest.
Arguments:
- volts: bfloat16 [16, 2, 1024, 18048], P('chan', None, 'stn'), may hold values from -6 to 6
- taps: float32 [16, 384], replicated, may hold values from -1.5 to 1.5
- survive: int32 [16, 8], replicated, may hold values from 0 to 383, as said below
- owner: int32 [16, 8], replicated, may hold values from 0 to 15, as said below
Outputs:
- visibilities: bfloat16 [16, 24, 2, 1024, 1024], P('chan', None, None, 'stn')
The draws below stay inside these ranges and needn't reach their ends.
Inputs may be any that keep to these rules, and one draw needn't show every extreme that they name: `survive`: each band lists 8 distinct fine channels. Within one band at most 2 channels share an owner, and in some band exactly 2 do; each owner holds at most 24 channels in all, and one owner holds exactly 24.
All inputs are finite; a program needn't handle non-finite values.
Results may differ from the reference program's by a relative error of at most 0.0076.
Values may be sent and summed in bfloat16 or wider, within the bound.
A program may use at most 128 MiB of HBM per device.

```python
import math
import jax
import jax.numpy as jnp
from jax import lax

FINE = 384
TAPS = 16
NSPEC = 32
KEEP = 8
RCAP = 24
CAP = 2
COARSE = 16
NINP = 1024
SAMP = 18048


def draw_survive(key, part):
    band_keys = jax.random.split(key, COARSE)
    return jax.vmap(lambda band_key: jax.random.permutation(band_key, FINE)[:KEEP])(band_keys).astype(jnp.int32)


def draw_owner(key, part):
    busy_key, shift_key, order_key = jax.random.split(key, 3)
    busy_owner = jax.random.randint(busy_key, (), 0, COARSE)
    busy_quota = RCAP // CAP
    busy_rest = RCAP % CAP
    window_width = min(busy_quota, COARSE)
    window_pick = jax.random.randint(shift_key, (), 0, window_width)
    rotation_offset = (busy_owner + COARSE // 2 - window_pick) % COARSE
    source_ids = jnp.arange(COARSE, dtype=jnp.int32)
    rotated = (source_ids - rotation_offset) % COARSE
    busy_count = jnp.where(rotated < busy_quota, CAP, jnp.where(rotated == busy_quota, busy_rest, 0))
    slot_ids = jnp.arange(KEEP, dtype=jnp.int32)
    leftover = slot_ids[None, :] - busy_count[:, None]
    other_owner = (busy_owner + 1 + (source_ids[:, None] + leftover + rotation_offset) % (COARSE - 1)) % COARSE
    base_owner = jnp.where(leftover < 0, busy_owner, other_owner)
    order_keys = jax.random.split(order_key, COARSE)
    orders = jax.vmap(lambda row_key: jax.random.permutation(row_key, KEEP))(order_keys)
    return jnp.take_along_axis(base_owner, orders, axis=1).astype(jnp.int32)


def level_of(key, shape, pieces, smallest, high):
    level = 1.0
    for position, shards_of in pieces:
        steps = jax.random.uniform(jax.random.fold_in(jax.random.fold_in(key, 6), position), (shards_of,), jnp.float32, smallest / len(pieces), high / len(pieces))
        level = level * jnp.repeat(jnp.exp(steps), shape[position] // shards_of).reshape((-1,) + (1,) * (len(shape) - 1 - position))
    return level


def bell_draw(stream_key, shape, scale, bound, cuts=(), kind=jnp.bfloat16):
    drawn = jax.random.normal(stream_key, shape, jnp.float32) * scale
    if len(cuts) > 0:
        drawn = level_of(stream_key, shape, cuts, -0.22, 0.18) * drawn
    return jnp.clip(drawn, min=-bound, max=bound).astype(kind)


def setup_inputs(seed: int = 0) -> dict:
    seeds = jax.random.split(jax.random.key(seed), 5)
    volts = bell_draw(seeds[0], (COARSE, 2, NINP, SAMP), 1.0, 6.0, ((0, 16), (2, 16)))
    taps = bell_draw(seeds[1], (TAPS, FINE), TAPS ** -0.5, 1.5, (), jnp.float32)
    survive = draw_survive(jax.random.fold_in(seeds[4], 71), 0)
    owner = draw_owner(jax.random.fold_in(seeds[4], 71), 0)
    return dict(volts=volts, taps=taps, survive=survive, owner=owner)


def fine_tables(chosen, fine_len):
    branch_ids = jnp.arange(fine_len, dtype=jnp.int32)
    phase_index = chosen[:, None] * branch_ids[None, :] % fine_len
    angles = phase_index.astype(jnp.float32) * (2.0 * math.pi / fine_len)
    factor = 1.0 / math.sqrt(fine_len)
    cosine = (jnp.cos(angles) * factor).astype(jnp.bfloat16)
    sine_table = (jnp.sin(angles) * factor).astype(jnp.bfloat16)
    return (cosine, sine_table)

def polyphase(signal, taps, spectra_count):
    accum = jnp.zeros((2, signal.shape[1], spectra_count, signal.shape[3]), jnp.float32)
    for tap_index in range(taps.shape[0]):
        accum = accum + taps[tap_index] * signal[:, :, tap_index:tap_index + spectra_count, :].astype(jnp.float32)
    return accum.astype(jnp.bfloat16)

def reference(volts, taps, survive, owner):

    def channelise(operands):
        band_volts, chosen = operands
        signal = band_volts.reshape(2, NINP, NSPEC + TAPS - 1, FINE)
        filtered = polyphase(signal, taps, NSPEC)
        cosine, sine_table = fine_tables(chosen, FINE)
        real_rows = filtered[0].reshape(NINP * NSPEC, FINE)
        imag_rows = filtered[1].reshape(NINP * NSPEC, FINE)
        real_part = jnp.dot(real_rows, cosine.T, preferred_element_type=jnp.float32) + jnp.dot(imag_rows, sine_table.T, preferred_element_type=jnp.float32)
        imag_part = jnp.dot(imag_rows, cosine.T, preferred_element_type=jnp.float32) - jnp.dot(real_rows, sine_table.T, preferred_element_type=jnp.float32)
        stacked = jnp.stack([real_part, imag_part]).astype(jnp.bfloat16).reshape(2, NINP, NSPEC, KEEP)
        return stacked.transpose(3, 2, 0, 1)
    spectra = lax.map(channelise, (volts, survive))
    flat = spectra.reshape(COARSE * KEEP, NSPEC, 2, NINP)

    def correlate(series):
        real_series = series[:, 0, :]
        imag_series = series[:, 1, :]
        real_part = jnp.dot(real_series.T, real_series, preferred_element_type=jnp.float32) + jnp.dot(imag_series.T, imag_series, preferred_element_type=jnp.float32)
        imag_part = jnp.dot(imag_series.T, real_series, preferred_element_type=jnp.float32) - jnp.dot(real_series.T, imag_series, preferred_element_type=jnp.float32)
        return (jnp.stack([real_part, imag_part]) / NSPEC).astype(jnp.bfloat16)
    grams = lax.map(correlate, flat)
    owners_flat = owner.reshape(-1)
    owner_hits = (owners_flat[:, None] == jnp.arange(COARSE, dtype=jnp.int32)[None, :]).astype(jnp.int32)
    owner_slot = lax.optimization_barrier(jnp.sum((jnp.cumsum(owner_hits, 0) - owner_hits) * owner_hits, 1))

    def place(slot_index):
        target = slot_index // RCAP
        within = slot_index % RCAP
        chosen_mask = ((owners_flat == target) & (owner_slot == within)).astype(jnp.int32)
        source = jnp.argmax(chosen_mask).astype(jnp.int32)
        present = jnp.max(chosen_mask)
        picked = lax.dynamic_index_in_dim(grams, source, 0, keepdims=False)
        return jnp.where(present > 0, picked, jnp.zeros_like(picked))
    visibilities = lax.map(place, jnp.arange(COARSE * RCAP, dtype=jnp.int32))
    return visibilities.reshape(COARSE, RCAP, 2, NINP, NINP)
```

```python
import functools
import math

import jax
import jax.numpy as jnp
from jax import lax
from jax.experimental import pallas as pl
from jax.experimental.pallas import tpu as pltpu
from jax.sharding import PartitionSpec as P

RCAP = 24
CAP = 2
FINE = 384
TAPS = 16
NSPEC = 32
KEEP = 8
NS = NSPEC + TAPS - 1
F32 = jnp.float32
BF16 = jnp.bfloat16
MESH = pl.DeviceIdType.MESH


def swap_halves(x):
    return pltpu.roll(x, 64, 1)


def trig_tables(chosen, branch):
    product = chosen * branch
    turns = jnp.floor((product + 0.5) * (1.0 / FINE))
    phase = product - turns * FINE
    quarter = jnp.floor((phase + (FINE // 8)) * (4.0 / FINE) + 1e-4)
    angle = (phase - quarter * (FINE // 4)) * (2.0 * math.pi / FINE)
    square = angle * angle
    sine = angle * (
        1.0
        + square
        * (-1.0 / 6 + square * (1.0 / 120 + square * (-1.0 / 5040 + square * (1.0 / 362880))))
    )
    cosine = 1.0 + square * (
        -0.5
        + square
        * (1.0 / 24 + square * (-1.0 / 720 + square * (1.0 / 40320 - square * (1.0 / 3628800))))
    )
    odd = (quarter == 1.0) | (quarter == 3.0)
    c = jnp.where(odd, sine, cosine)
    s = jnp.where(odd, cosine, sine)
    c = jnp.where((quarter == 1.0) | (quarter == 2.0), -c, c)
    s = jnp.where((quarter == 2.0) | (quarter == 3.0), -s, s)
    factor = 1.0 / math.sqrt(FINE)
    return ((c * factor).astype(BF16).astype(F32), (s * factor).astype(BF16).astype(F32))


CHUNKS = ((0, 12), (12, 24), (24, 36), (36, NS))


def channelise_kernel(
    survive_ref, owner_ref, taps_ref, volts_ref, out_ref, index_ref, buf, weights, partial, rows, sems
):
    band = lax.axis_index("chan")
    copies = []
    for n, (lo, hi) in enumerate(CHUNKS):
        copy = pltpu.make_async_copy(
            volts_ref.at[0, :, :, lo * FINE : hi * FINE],
            buf.at[:, :, lo * FINE : hi * FINE],
            sems.at[n],
        )
        copy.start()
        copies.append(copy)

    count = jnp.int32(0)
    for b in range(owner_ref.shape[0]):
        start = count
        for j in range(KEEP):
            hit = (owner_ref[b, j] == band).astype(jnp.int32)
            index_ref[jnp.minimum(count, RCAP)] = b * CAP + count - start
            count = count + hit
    index_ref[RCAP + 1] = count

    row = lax.broadcasted_iota(jnp.int32, (KEEP, FINE), 0)
    branch = lax.broadcasted_iota(jnp.int32, (KEEP, FINE), 1).astype(F32)
    chosen = jnp.zeros((KEEP, FINE), jnp.int32)
    for j in range(KEEP):
        chosen = jnp.where(row == j, survive_ref[band, j], chosen)
    cosine, sine = trig_tables(chosen.astype(F32), branch)
    both = jnp.concatenate([cosine, sine], 0)
    for p in range(TAPS):
        weights[p * 16 : (p + 1) * 16, :] = (both * taps_ref[p : p + 1, :]).astype(BF16)

    lane = lax.broadcasted_iota(jnp.int32, (KEEP, 128), 1)

    def finish(t):
        total = partial[t, 0:16, :]
        for p in range(1, TAPS):
            total = total + partial[t + p, p * 16 : (p + 1) * 16, :]
        swapped = swap_halves(total[8:16])
        rows[pl.ds(t, KEEP, stride=NSPEC), :] = total[0:8] + jnp.where(lane < 64, swapped, -swapped)

    done = 0
    for n, (lo, hi) in enumerate(CHUNKS):
        copies[n].wait()
        s = lo
        while s < hi:
            width = min(2, hi - s)
            block = jnp.concatenate(
                [
                    buf[:, :, (s + u) * FINE : (s + u + 1) * FINE].reshape(128, FINE)
                    for u in range(width)
                ],
                0,
            )
            product = lax.dot_general(
                weights[...], block, (((1,), (1,)), ((), ())), preferred_element_type=F32
            )
            for u in range(width):
                partial[s + u] = product[:, u * 128 : (u + 1) * 128]
            s += width
            while done + TAPS <= s and done < NSPEC:
                finish(done)
                done += 1

    out_ref[...] = jnp.zeros_like(out_ref)
    for j in range(KEEP):
        mine = owner_ref[band, j]
        rank = jnp.int32(0)
        for other in range(j):
            rank = rank + (owner_ref[band, other] == mine).astype(jnp.int32)
        out_ref[mine * CAP + rank] = rows[j * NSPEC : (j + 1) * NSPEC, :].astype(BF16)


def channelise(volts, taps, survive, owner):
    inputs = volts.shape[2]
    return pl.pallas_call(
        channelise_kernel,
        out_shape=(
            jax.ShapeDtypeStruct((owner.shape[0] * CAP, NSPEC, 2 * inputs), BF16),
            jax.ShapeDtypeStruct((RCAP + 8,), jnp.int32),
        ),
        in_specs=[
            pl.BlockSpec(memory_space=pltpu.SMEM),
            pl.BlockSpec(memory_space=pltpu.SMEM),
            pl.BlockSpec(memory_space=pltpu.VMEM),
            pl.BlockSpec(memory_space=pl.ANY),
        ],
        out_specs=(
            pl.BlockSpec(memory_space=pltpu.VMEM),
            pl.BlockSpec(memory_space=pltpu.SMEM),
        ),
        scratch_shapes=[
            pltpu.VMEM((2, inputs, NS * FINE), BF16),
            pltpu.VMEM((TAPS * 16, FINE), BF16),
            pltpu.VMEM((NS, TAPS * 16, 2 * inputs), F32),
            pltpu.VMEM((KEEP * NSPEC, 2 * inputs), F32),
            pltpu.SemaphoreType.DMA((len(CHUNKS),)),
        ],
        compiler_params=pltpu.CompilerParams(vmem_limit_bytes=58 << 20),
        name="channelise",
    )(survive, owner, taps, volts)


KCH = 4
PER = RCAP // KCH
OWN, Y0, R0, L0, R1, L1, F0, F1 = range(8)


def exchange_kernel(
    index_ref, out_ref, gathered, arrived, send1, recv1, send2, recv2, sib_send, sib_recv
):
    stn = lax.axis_index("stn")
    chan = lax.axis_index("chan")
    nchan = lax.axis_size("chan")
    x, y, core = stn // 4, (stn // 2) % 2, stn % 2

    def name(dx, dy, dcore=0):
        return ((x + dx) % 4) * 4 + ((y + dy) % 2) * 2 + (core + dcore) % 2

    places = {
        OWN: (0, 0), Y0: (0, 1), R0: (1, 0), L0: (3, 0), R1: (1, 1), L1: (3, 1), F0: (2, 0), F1: (2, 1)
    }
    right, left, across, sibling = name(1, 0), name(3, 0), name(0, 1), name(0, 0, 1)

    barrier = pltpu.get_barrier_semaphore()
    for other in (right, left, across, sibling):
        pl.semaphore_signal(
            barrier, inc=1, device_id={"stn": other, "chan": chan}, device_id_type=MESH
        )
    for step in range(1, nchan):
        pl.semaphore_signal(
            barrier,
            inc=1,
            device_id={"stn": stn, "chan": (chan + step) % nchan},
            device_id_type=MESH,
        )
    pl.semaphore_wait(barrier, 4 + nchan - 1)

    def turn(step):
        to = (chan + step) % nchan
        return pltpu.make_async_remote_copy(
            src_ref=out_ref.at[pl.ds(to * CAP, CAP)],
            dst_ref=arrived.at[pl.ds(chan * CAP, CAP)],
            send_sem=send1.at[step],
            recv_sem=recv1.at[step],
            device_id={"stn": stn, "chan": to},
            device_id_type=MESH,
        )

    order = [s for d in range(nchan // 2, 0, -1) for s in sorted({d, nchan - d})]
    turns = {s: turn(s) for s in order}
    for s in order:
        turns[s].start()
    arrived[pl.ds(chan * CAP, CAP)] = out_ref[pl.ds(chan * CAP, CAP)]
    for s in order:
        turns[s].wait_recv()

    count = index_ref[RCAP + 1]
    for r in range(RCAP):
        block = arrived[index_ref[r] % (nchan * CAP)]
        gathered[stn, r] = jnp.where(r < count, block, jnp.zeros_like(block))

    sends = []

    def part(block, k):
        dx, dy = places[block]
        return gathered.at[name(dx, dy), pl.ds(k * PER, PER)]

    def push(block, k, to, slot):
        copy = pltpu.make_async_remote_copy(
            src_ref=part(block, k),
            dst_ref=part(block, k),
            send_sem=send2.at[slot, k],
            recv_sem=recv2.at[slot, k],
            device_id={"stn": to, "chan": chan},
            device_id_type=MESH,
        )
        copy.start()
        sends.append(copy)

    def share(block, k):
        copy = pltpu.make_async_remote_copy(
            src_ref=part(block, k),
            dst_ref=part(block, k),
            send_sem=sib_send.at[block, k],
            recv_sem=sib_recv.at[block, k],
            device_id={"stn": sibling, "chan": chan},
            device_id_type=MESH,
        )
        copy.start()
        sends.append(copy)

    def arrive(block, k):
        pltpu.make_async_remote_copy(
            src_ref=part(block, k),
            dst_ref=part(block, k),
            send_sem=send2.at[block, k],
            recv_sem=recv2.at[block, k],
            device_id={"stn": right, "chan": chan},
            device_id_type=MESH,
        ).wait_recv()

    for k in range(KCH):
        push(OWN, k, across, Y0)
        push(OWN, k, right, L0)
        push(OWN, k, left, R0)
        share(OWN, k)
    for k in range(KCH):
        arrive(Y0, k)
        push(Y0, k, right, L1)
        push(Y0, k, left, R1)
        share(Y0, k)
        arrive(R0, k)
        if k < KCH // 2:
            push(R0, k, left, F0)
        share(R0, k)
        arrive(L0, k)
        if k >= KCH // 2:
            push(L0, k, right, F0)
        share(L0, k)
    for k in (v for pair in zip(range(KCH // 2), range(KCH // 2, KCH)) for v in pair):
        arrive(F0, k)
        push(F0, k, across, F1)
        share(F0, k)
    for k in range(KCH):
        arrive(R1, k)
        share(R1, k)
        arrive(L1, k)
        share(L1, k)
    for k in range(KCH):
        arrive(F1, k)
        share(F1, k)
    for block in range(8):
        dx, dy = places[block]
        for k in range(KCH):
            ref = gathered.at[name(dx, dy, 1), pl.ds(k * PER, PER)]
            pltpu.make_async_remote_copy(
                src_ref=ref,
                dst_ref=ref,
                send_sem=sib_send.at[block, k],
                recv_sem=sib_recv.at[block, k],
                device_id={"stn": sibling, "chan": chan},
                device_id_type=MESH,
            ).wait_recv()
    for s in order:
        turns[s].wait_send()
    for copy in sends:
        copy.wait_send()


def exchange(index, outgoing, stn_count):
    slots, spectra, lanes = outgoing.shape
    return pl.pallas_call(
        exchange_kernel,
        out_shape=jax.ShapeDtypeStruct((stn_count, RCAP, spectra, lanes), BF16),
        in_specs=[
            pl.BlockSpec(memory_space=pltpu.SMEM),
            pl.BlockSpec(memory_space=pltpu.VMEM),
        ],
        out_specs=pl.BlockSpec(memory_space=pltpu.VMEM),
        scratch_shapes=[
            pltpu.VMEM((slots, spectra, lanes), BF16),
            pltpu.SemaphoreType.DMA((slots // CAP,)),
            pltpu.SemaphoreType.DMA((slots // CAP,)),
            pltpu.SemaphoreType.DMA((8, KCH)),
            pltpu.SemaphoreType.DMA((8, KCH)),
            pltpu.SemaphoreType.DMA((8, KCH)),
            pltpu.SemaphoreType.DMA((8, KCH)),
        ],
        compiler_params=pltpu.CompilerParams(
            collective_id=0, has_side_effects=True, vmem_limit_bytes=16 << 20
        ),
        name="exchange",
    )(index, outgoing)


SLOTS_STEP = 2


def correlate_kernel(stn_count, spectra_count, gathered, out_ref):
    stn = lax.axis_index("stn")
    step = pl.program_id(0)
    lane = lax.broadcasted_iota(jnp.int32, (spectra_count, 128), 1)
    low = lane < 64
    for u in range(SLOTS_STEP):
        slot = step * SLOTS_STEP + u
        own = gathered[stn, slot].astype(F32) * (1.0 / spectra_count)
        turned = swap_halves(own)
        turned = jnp.where(low, turned, -turned)
        left = jnp.concatenate([own, turned], 0).astype(BF16)
        for n in range(0, stn_count, 2):
            first = gathered[n, slot].astype(F32)
            second = gathered[n + 1, slot].astype(F32)
            real = jnp.where(low, first, swap_halves(second))
            imag = jnp.where(low, swap_halves(first), second)
            block = jnp.concatenate([real, imag], 0).astype(BF16)
            product = lax.dot_general(
                left, block, (((0,), (0,)), ((), ())), preferred_element_type=F32
            )
            out_ref[0, u, :, :, n * 64 : (n + 2) * 64] = product.astype(BF16).reshape(2, 64, 128)


def correlate(gathered):
    stn_count, slots, spectra, lanes = gathered.shape
    inputs = lanes // 2
    return pl.pallas_call(
        functools.partial(correlate_kernel, stn_count, spectra),
        grid=(slots // SLOTS_STEP,),
        out_shape=jax.ShapeDtypeStruct((1, slots, 2, inputs, stn_count * inputs), BF16),
        in_specs=[pl.BlockSpec(memory_space=pltpu.VMEM)],
        out_specs=pl.BlockSpec(
            (1, SLOTS_STEP, 2, inputs, stn_count * inputs), lambda i: (0, i, 0, 0, 0)
        ),
        compiler_params=pltpu.CompilerParams(vmem_limit_bytes=16 << 20),
        name="correlate",
    )(gathered)


def per_device(volts, taps, survive, owner):
    outgoing, index = channelise(volts, taps, survive, owner)
    gathered = exchange(index, outgoing, lax.axis_size("stn"))
    return correlate(gathered)


def solution(mesh):
    return jax.shard_map(
        per_device,
        mesh=mesh,
        in_specs=(P("chan", None, "stn", None), P(), P(), P()),
        out_specs=P("chan", None, None, "stn", None),
        check_vma=False,
    )
```

```python
import functools
import math

import jax
import jax.numpy as jnp
from jax import lax
from jax.experimental import pallas as pl
from jax.experimental.pallas import tpu as pltpu
from jax.sharding import PartitionSpec as P

RCAP = 24
CAP = 2
FINE = 384
TAPS = 16
NSPEC = 32
KEEP = 8
NS = NSPEC + TAPS - 1
F32 = jnp.float32
BF16 = jnp.bfloat16
MESH = pl.DeviceIdType.MESH


def swap_halves(x):
    return pltpu.roll(x, 64, 1)


def trig_tables(chosen, branch):
    product = chosen * branch
    turns = jnp.floor((product + 0.5) * (1.0 / FINE))
    phase = product - turns * FINE
    quarter = jnp.floor((phase + (FINE // 8)) * (4.0 / FINE) + 1e-4)
    angle = (phase - quarter * (FINE // 4)) * (2.0 * math.pi / FINE)
    square = angle * angle
    sine = angle * (
        1.0
        + square
        * (-1.0 / 6 + square * (1.0 / 120 + square * (-1.0 / 5040 + square * (1.0 / 362880))))
    )
    cosine = 1.0 + square * (
        -0.5
        + square
        * (1.0 / 24 + square * (-1.0 / 720 + square * (1.0 / 40320 - square * (1.0 / 3628800))))
    )
    odd = (quarter == 1.0) | (quarter == 3.0)
    c = jnp.where(odd, sine, cosine)
    s = jnp.where(odd, cosine, sine)
    c = jnp.where((quarter == 1.0) | (quarter == 2.0), -c, c)
    s = jnp.where((quarter == 2.0) | (quarter == 3.0), -s, s)
    factor = 1.0 / math.sqrt(FINE)
    return ((c * factor).astype(BF16).astype(F32), (s * factor).astype(BF16).astype(F32))


STEP = 4
STEPS = (NS + STEP) // STEP
HALVES = 2
HALF = NSPEC // HALVES
KS = 2
PER = RCAP // KS
KCH = HALVES * KS
OWN, Y0, R0, L0, R1, L1, F0, F1 = range(8)
PLACES = {
    OWN: (0, 0), Y0: (0, 1), R0: (1, 0), L0: (3, 0), R1: (1, 1), L1: (3, 1), F0: (2, 0), F1: (2, 1)
}


def front_kernel(
    survive_ref, owner_ref, taps_ref, volts_ref, gathered,
    buf, weights, partial, rows, channels, outbox, arrived0, arrived1, pick, source,
    load_sem, send1, recv1, send2, recv2, sib_send, sib_recv,
):
    arrived = (arrived0, arrived1)
    stn = lax.axis_index("stn")
    chan = lax.axis_index("chan")
    nchan = lax.axis_size("chan")
    x, y, core = stn // 4, (stn // 2) % 2, stn % 2

    def name(dx, dy, dcore=0):
        return ((x + dx) % 4) * 4 + ((y + dy) % 2) * 2 + (core + dcore) % 2

    right, left, across, sibling = name(1, 0), name(3, 0), name(0, 1), name(0, 0, 1)

    def load(n, width=STEP):
        lanes = pl.ds(pl.multiple_of(n * (STEP * FINE), 128), width * FINE)
        return pltpu.make_async_copy(
            volts_ref.at[0, :, :, lanes], buf.at[:, :, lanes], load_sem.at[n]
        )

    last = NS - (STEPS - 1) * STEP

    @pl.loop(0, STEPS - 1)
    def _(n):
        load(n).start()

    load(STEPS - 1, last).start()

    barrier = pltpu.get_barrier_semaphore()
    for other in (right, left, across, sibling):
        pl.semaphore_signal(
            barrier, inc=1, device_id={"stn": other, "chan": chan}, device_id_type=MESH
        )

    @pl.loop(1, nchan)
    def _(step):
        pl.semaphore_signal(
            barrier,
            inc=1,
            device_id={"stn": stn, "chan": (chan + step) % nchan},
            device_id_type=MESH,
        )

    row = lax.broadcasted_iota(jnp.int32, (KEEP, FINE), 0)
    branch = lax.broadcasted_iota(jnp.int32, (KEEP, FINE), 1).astype(F32)
    chosen = jnp.zeros((KEEP, FINE), jnp.int32)
    for j in range(KEEP):
        chosen = jnp.where(row == j, survive_ref[j, chan], chosen)
    cosine, sine = trig_tables(chosen.astype(F32), branch)
    both = jnp.concatenate([cosine, sine], 0)
    for p in range(TAPS):
        weights[p * 16 : (p + 1) * 16, :] = (both * taps_ref[p : p + 1, :]).astype(BF16)

    targets = []
    owners = [owner_ref[j, chan] for j in range(KEEP)]
    for j in range(KEEP):
        rank = jnp.int32(0)
        for other in range(j):
            rank = rank + (owners[other] == owners[j]).astype(jnp.int32)
        targets.append(owners[j] * CAP + rank)

    @pl.loop(0, nchan * CAP)
    def _(slot):
        found = jnp.int32(0)
        for j in range(1, KEEP):
            found = jnp.where(targets[j] == slot, j, found)
        pick[slot] = found

    def transform(n):
        at = n * (STEP * FINE)
        for pair in range(STEP // 2):
            block = jnp.concatenate(
                [
                    buf[:, :, pl.ds(pl.multiple_of(at + (pair * 2 + u) * FINE, 128), FINE)].reshape(
                        128, FINE
                    )
                    for u in range(2)
                ],
                0,
            )
            product = lax.dot_general(
                weights[...], block, (((1,), (1,)), ((), ())), preferred_element_type=F32
            )
            for u in range(2):
                partial[n * STEP + pair * 2 + u] = product[:, u * 128 : (u + 1) * 128]

    lane = lax.broadcasted_iota(jnp.int32, (KEEP, 128), 1)

    def turn(half, step):
        to = (chan + step) % nchan
        return pltpu.make_async_remote_copy(
            src_ref=outbox.at[half, pl.ds(to * CAP, CAP)],
            dst_ref=arrived[half].at[pl.ds(chan * CAP, CAP)],
            send_sem=send1.at[half, step],
            recv_sem=recv1.at[half, step],
            device_id={"stn": stn, "chan": to},
            device_id_type=MESH,
        )

    done = 0
    for half in range(HALVES):
        upto = ((half + 1) * HALF + TAPS - 1 + STEP - 1) // STEP

        @pl.loop(done, upto)
        def _(n):
            @pl.when(n < STEPS - 1)
            def _():
                load(n).wait()

            @pl.when(n == STEPS - 1)
            def _():
                load(STEPS - 1, last).wait()

            transform(n)

        done = upto

        @pl.loop(0, HALF)
        def _(t):
            at = half * HALF + t
            total = partial[at, 0:16, :]
            for p in range(1, TAPS):
                total = total + partial[at + p, p * 16 : (p + 1) * 16, :]
            swapped = swap_halves(total[8:16])
            rows[pl.ds(t, KEEP, stride=HALF), :] = total[0:8] + jnp.where(
                lane < 64, swapped, -swapped
            )

        for j in range(KEEP):
            channels[j] = rows[j * HALF : (j + 1) * HALF, :].astype(BF16)

        @pl.loop(0, nchan * CAP)
        def _(slot):
            outbox[half, slot] = channels[pick[slot]]

        if half == 0:
            pl.semaphore_wait(barrier, 4 + nchan - 1)

        @pl.loop(0, nchan - 1)
        def _(i):
            turn(half, nchan // 2 + ((i + 1) // 2) * (2 * (i % 2) - 1)).start()

        arrived[half][pl.ds(chan * CAP, CAP)] = outbox[half, pl.ds(chan * CAP, CAP)]

    counts = []
    count = jnp.int32(0)
    for b in range(nchan):
        for j in range(KEEP):
            count = count + (owner_ref[j, b] == chan).astype(jnp.int32)
        counts.append(count)

    @pl.loop(0, RCAP)
    def _(r):
        skip = jnp.int32(0)
        for b in range(nchan):
            skip = jnp.where(counts[b] <= r, (b + 1) * CAP - counts[b], skip)
        source[r] = jnp.minimum(r + skip, nchan * CAP - 1)

    sends = []

    def part(block, k):
        dx, dy = PLACES[block]
        return gathered.at[k // KS, name(dx, dy), pl.ds((k % KS) * PER, PER)]

    def whole(block, half, dcore=0):
        dx, dy = PLACES[block]
        return gathered.at[half, name(dx, dy, dcore)]

    def push(block, k, to, slot):
        copy = pltpu.make_async_remote_copy(
            src_ref=part(block, k),
            dst_ref=part(block, k),
            send_sem=send2.at[slot, k],
            recv_sem=recv2.at[slot, k],
            device_id={"stn": to, "chan": chan},
            device_id_type=MESH,
        )
        copy.start()
        sends.append(copy)

    def share(block, k):
        if k % KS < KS - 1:
            return
        copy = pltpu.make_async_remote_copy(
            src_ref=whole(block, k // KS),
            dst_ref=whole(block, k // KS),
            send_sem=sib_send.at[block, k // KS],
            recv_sem=sib_recv.at[block, k // KS],
            device_id={"stn": sibling, "chan": chan},
            device_id_type=MESH,
        )
        copy.start()
        sends.append(copy)

    def arrive(block, k):
        pltpu.make_async_remote_copy(
            src_ref=part(block, k),
            dst_ref=part(block, k),
            send_sem=send2.at[block, k],
            recv_sem=recv2.at[block, k],
            device_id={"stn": right, "chan": chan},
            device_id_type=MESH,
        ).wait_recv()

    for half in range(HALVES):

        @pl.loop(1, nchan)
        def _(step):
            turn(half, step).wait_recv()

        @pl.loop(0, RCAP)
        def _(r):
            block = arrived[half][source[r]]
            gathered[half, stn, r] = jnp.where(r < count, block, jnp.zeros_like(block))

        for k in range(half * KS, (half + 1) * KS):
            push(OWN, k, right, L0)
            push(OWN, k, left, R0)
            push(OWN, k, across, Y0)
            share(OWN, k)

    def far(k):
        arrive(F0, k)
        push(F0, k, across, F1)
        share(F0, k)

    for k in range(KCH):
        arrive(R0, k)
        if k % 2 == 0:
            push(R0, k, left, F0)
        arrive(L0, k)
        if k % 2 == 1:
            push(L0, k, right, F0)
        arrive(Y0, k)
        push(Y0, k, right, L1)
        push(Y0, k, left, R1)
        for block in (R0, L0, Y0):
            share(block, k)
        if k >= 2:
            far(k - 2)
    for k in range(KCH - 2, KCH):
        far(k)
    for k in range(KCH):
        arrive(R1, k)
        share(R1, k)
        arrive(L1, k)
        share(L1, k)
    for k in range(KCH):
        arrive(F1, k)
        share(F1, k)
    for block in range(8):
        for half in range(HALVES):
            pltpu.make_async_remote_copy(
                src_ref=whole(block, half, 1),
                dst_ref=whole(block, half, 1),
                send_sem=sib_send.at[block, half],
                recv_sem=sib_recv.at[block, half],
                device_id={"stn": sibling, "chan": chan},
                device_id_type=MESH,
            ).wait_recv()
    for half in range(HALVES):

        @pl.loop(1, nchan)
        def _(step):
            turn(half, step).wait_send()

    for copy in sends:
        copy.wait_send()


def front(volts, taps, survive, owner, stn_count):
    inputs = volts.shape[2]
    lanes = 2 * inputs
    nchan = owner.shape[1]
    dma = pltpu.SemaphoreType.DMA
    return pl.pallas_call(
        front_kernel,
        out_shape=jax.ShapeDtypeStruct((HALVES, stn_count, RCAP, HALF, lanes), BF16),
        in_specs=[
            pl.BlockSpec(memory_space=pltpu.SMEM),
            pl.BlockSpec(memory_space=pltpu.SMEM),
            pl.BlockSpec(memory_space=pltpu.VMEM),
            pl.BlockSpec(memory_space=pltpu.HBM),
        ],
        out_specs=pl.BlockSpec(memory_space=pltpu.VMEM),
        scratch_shapes=[
            pltpu.VMEM((2, inputs, STEPS * STEP * FINE), BF16),
            pltpu.VMEM((TAPS * 16, FINE), BF16),
            pltpu.VMEM((STEPS * STEP, TAPS * 16, lanes), F32),
            pltpu.VMEM((KEEP * HALF, lanes), F32),
            pltpu.VMEM((KEEP, HALF, lanes), BF16),
            pltpu.VMEM((HALVES, nchan * CAP, HALF, lanes), BF16),
            pltpu.VMEM((nchan * CAP, HALF, lanes), BF16),
            pltpu.VMEM((nchan * CAP, HALF, lanes), BF16),
            pltpu.SMEM((nchan * CAP,), jnp.int32),
            pltpu.SMEM((RCAP,), jnp.int32),
            dma((STEPS,)),
            dma((HALVES, nchan)),
            dma((HALVES, nchan)),
            dma((8, KCH)),
            dma((8, KCH)),
            dma((8, HALVES)),
            dma((8, HALVES)),
        ],
        compiler_params=pltpu.CompilerParams(
            collective_id=0, has_side_effects=True, vmem_limit_bytes=48 << 20
        ),
        name="front",
    )(survive, owner, taps, volts)


def correlate_kernel(stn_count, gathered, out_ref, built, sems):
    stn = lax.axis_index("stn")
    low = lax.broadcasted_iota(jnp.int32, (NSPEC, 128), 1) < 64

    def series(n, slot):
        return jnp.concatenate([gathered[h, n, slot] for h in range(HALVES)], 0).astype(F32)

    def store(slot):
        return pltpu.make_async_copy(built.at[slot], out_ref.at[0, slot], sems.at[slot])

    @pl.loop(0, RCAP)
    def _(slot):
        own = series(stn, slot) * (1.0 / NSPEC)
        turned = swap_halves(own)
        turned = jnp.where(low, turned, -turned)
        left = jnp.concatenate([own, turned], 0).astype(BF16)
        for n in range(0, stn_count, 4):
            columns = []
            for m in range(n, n + 4, 2):
                first, second = series(m, slot), series(m + 1, slot)
                real = jnp.where(low, first, swap_halves(second))
                imag = jnp.where(low, swap_halves(first), second)
                columns.append(jnp.concatenate([real, imag], 0).astype(BF16))
            product = lax.dot_general(
                left,
                jnp.concatenate(columns, 1),
                (((0,), (0,)), ((), ())),
                preferred_element_type=F32,
            )
            built[slot, :, :, n * 64 : (n + 4) * 64] = product.astype(BF16).reshape(2, 64, 256)
        store(slot).start()

    @pl.loop(0, RCAP)
    def _(slot):
        store(slot).wait()


def correlate(gathered):
    stn_count, lanes = gathered.shape[1], gathered.shape[4]
    inputs = lanes // 2
    return pl.pallas_call(
        functools.partial(correlate_kernel, stn_count),
        out_shape=jax.ShapeDtypeStruct((1, RCAP, 2, inputs, stn_count * inputs), BF16),
        in_specs=[pl.BlockSpec(memory_space=pltpu.VMEM)],
        out_specs=pl.BlockSpec(memory_space=pltpu.HBM),
        scratch_shapes=[
            pltpu.VMEM((RCAP, 2, inputs, stn_count * inputs), BF16),
            pltpu.SemaphoreType.DMA((RCAP,)),
        ],
        compiler_params=pltpu.CompilerParams(vmem_limit_bytes=16 << 20),
        name="correlate",
    )(gathered)


def per_device(volts, taps, survive, owner):
    gathered = front(volts, taps, survive.T, owner.T, lax.axis_size("stn"))
    return correlate(gathered)


def solution(mesh):
    return jax.shard_map(
        per_device,
        mesh=mesh,
        in_specs=(P("chan", None, "stn", None), P(), P(), P()),
        out_specs=P("chan", None, None, "stn", None),
        check_vma=False,
    )
```

```python
import functools
import math

import jax
import jax.numpy as jnp
from jax import lax
from jax.experimental import pallas as pl
from jax.experimental.pallas import tpu as pltpu
from jax.sharding import PartitionSpec as P

RCAP = 24
CAP = 2
FINE = 384
TAPS = 16
NSPEC = 32
KEEP = 8
NS = NSPEC + TAPS - 1
F32 = jnp.float32
BF16 = jnp.bfloat16
MESH = pl.DeviceIdType.MESH


def swap_halves(x):
    return pltpu.roll(x, 64, 1)


def trig_tables(chosen, branch):
    product = chosen * branch
    turns = jnp.floor((product + 0.5) * (1.0 / FINE))
    phase = product - turns * FINE
    quarter = jnp.floor((phase + (FINE // 8)) * (4.0 / FINE) + 1e-4)
    angle = (phase - quarter * (FINE // 4)) * (2.0 * math.pi / FINE)
    square = angle * angle
    sine = angle * (
        1.0
        + square
        * (-1.0 / 6 + square * (1.0 / 120 + square * (-1.0 / 5040 + square * (1.0 / 362880))))
    )
    cosine = 1.0 + square * (
        -0.5
        + square
        * (1.0 / 24 + square * (-1.0 / 720 + square * (1.0 / 40320 - square * (1.0 / 3628800))))
    )
    odd = (quarter == 1.0) | (quarter == 3.0)
    c = jnp.where(odd, sine, cosine)
    s = jnp.where(odd, cosine, sine)
    c = jnp.where((quarter == 1.0) | (quarter == 2.0), -c, c)
    s = jnp.where((quarter == 2.0) | (quarter == 3.0), -s, s)
    factor = 1.0 / math.sqrt(FINE)
    return ((c * factor).astype(BF16).astype(F32), (s * factor).astype(BF16).astype(F32))


CHUNKS = ((0, 11), (11, 21), (21, 31), (31, 39), (39, NS))
SLOTS_STEP = 8
HALVES = 2
HALF = NSPEC // HALVES
KS = 2
PER = RCAP // KS
KCH = HALVES * KS
OWN, Y0, R0, L0, R1, L1, F0, F1 = range(8)
PLACES = {
    OWN: (0, 0), Y0: (0, 1), R0: (1, 0), L0: (3, 0), R1: (1, 1), L1: (3, 1), F0: (2, 0), F1: (2, 1)
}


def front_kernel(
    survive_ref, owner_ref, taps_ref, volts_ref, gathered,
    buf, weights, partial, rows, channels, outbox, arrived0, arrived1, pick, source,
    load_sem, send1, recv1, send2, recv2, sib_send, sib_recv,
):
    arrived = (arrived0, arrived1)
    stn = lax.axis_index("stn")
    chan = lax.axis_index("chan")
    nchan = lax.axis_size("chan")
    x, y, core = stn // 4, (stn // 2) % 2, stn % 2

    def name(dx, dy, dcore=0):
        return ((x + dx) % 4) * 4 + ((y + dy) % 2) * 2 + (core + dcore) % 2

    right, left, across, sibling = name(1, 0), name(3, 0), name(0, 1), name(0, 0, 1)

    def load(n):
        lanes = pl.ds(CHUNKS[n][0] * FINE, (CHUNKS[n][1] - CHUNKS[n][0]) * FINE)
        return pltpu.make_async_copy(
            volts_ref.at[0, :, :, lanes], buf.at[:, :, lanes], load_sem.at[n]
        )

    for n in range(len(CHUNKS)):
        load(n).start()

    barrier = pltpu.get_barrier_semaphore()
    for other in (right, left, across, sibling):
        pl.semaphore_signal(
            barrier, inc=1, device_id={"stn": other, "chan": chan}, device_id_type=MESH
        )

    @pl.loop(1, nchan)
    def _(step):
        pl.semaphore_signal(
            barrier,
            inc=1,
            device_id={"stn": stn, "chan": (chan + step) % nchan},
            device_id_type=MESH,
        )

    row = lax.broadcasted_iota(jnp.int32, (KEEP, FINE), 0)
    branch = lax.broadcasted_iota(jnp.int32, (KEEP, FINE), 1).astype(F32)
    chosen = jnp.zeros((KEEP, FINE), jnp.int32)
    for j in range(KEEP):
        chosen = jnp.where(row == j, survive_ref[j, chan], chosen)
    cosine, sine = trig_tables(chosen.astype(F32), branch)
    both = jnp.concatenate([cosine, sine], 0)
    for p in range(TAPS):
        weights[p * 16 : (p + 1) * 16, :] = (both * taps_ref[p : p + 1, :]).astype(BF16)

    targets = []
    owners = [owner_ref[j, chan] for j in range(KEEP)]
    for j in range(KEEP):
        rank = jnp.int32(0)
        for other in range(j):
            rank = rank + (owners[other] == owners[j]).astype(jnp.int32)
        targets.append(owners[j] * CAP + rank)

    for slot in range(nchan * CAP):
        found = jnp.int32(0)
        for j in range(1, KEEP):
            found = jnp.where(targets[j] == slot, j, found)
        pick[slot] = found

    def transform(first, width):
        block = jnp.concatenate(
            [
                buf[:, :, (first + u) * FINE : (first + u + 1) * FINE].reshape(128, FINE)
                for u in range(width)
            ],
            0,
        )
        product = lax.dot_general(
            weights[...], block, (((1,), (1,)), ((), ())), preferred_element_type=F32
        )
        for u in range(width):
            partial[first + u] = product[:, u * 128 : (u + 1) * 128]

    def finish(t):
        total = partial[t, 0:16, :]
        for p in range(1, TAPS):
            total = total + partial[t + p, p * 16 : (p + 1) * 16, :]
        swapped = swap_halves(total[8:16])
        rows[pl.ds(t % HALF, KEEP, stride=HALF), :] = total[0:8] + jnp.where(
            lane < 64, swapped, -swapped
        )

    lane = lax.broadcasted_iota(jnp.int32, (KEEP, 128), 1)

    def turn(half, step):
        to = (chan + step) % nchan
        return pltpu.make_async_remote_copy(
            src_ref=outbox.at[half, pl.ds(to * CAP, CAP)],
            dst_ref=arrived[half].at[pl.ds(chan * CAP, CAP)],
            send_sem=send1.at[half, step],
            recv_sem=recv1.at[half, step],
            device_id={"stn": stn, "chan": to},
            device_id_type=MESH,
        )

    chunk = 0
    done = 0
    for half in range(HALVES):
        while done < (half + 1) * HALF:
            load(chunk).wait()
            lo, hi = CHUNKS[chunk]
            chunk += 1
            for first in range(lo, hi, 2):
                width = min(2, hi - first)
                transform(first, width)
                while done + TAPS <= first + width and done < (half + 1) * HALF:
                    finish(done)
                    done += 1

        for j in range(KEEP):
            channels[j] = rows[j * HALF : (j + 1) * HALF, :].astype(BF16)

        for slot in range(nchan * CAP):
            outbox[half, slot] = channels[pick[slot]]

        if half == 0:
            pl.semaphore_wait(barrier, 4 + nchan - 1)

        @pl.loop(0, nchan - 1)
        def _(i):
            turn(half, nchan // 2 + ((i + 1) // 2) * (2 * (i % 2) - 1)).start()

        arrived[half][pl.ds(chan * CAP, CAP)] = outbox[half, pl.ds(chan * CAP, CAP)]

    counts = []
    count = jnp.int32(0)
    for b in range(nchan):
        for j in range(KEEP):
            count = count + (owner_ref[j, b] == chan).astype(jnp.int32)
        counts.append(count)

    @pl.loop(0, RCAP)
    def _(r):
        skip = jnp.int32(0)
        for b in range(nchan):
            skip = jnp.where(counts[b] <= r, (b + 1) * CAP - counts[b], skip)
        source[r] = jnp.minimum(r + skip, nchan * CAP - 1)

    sends = []

    def part(block, k):
        dx, dy = PLACES[block]
        return gathered.at[k // KS, name(dx, dy), pl.ds((k % KS) * PER, PER)]

    def whole(block, half, dcore=0):
        dx, dy = PLACES[block]
        return gathered.at[half, name(dx, dy, dcore)]

    def push(block, k, to, slot):
        copy = pltpu.make_async_remote_copy(
            src_ref=part(block, k),
            dst_ref=part(block, k),
            send_sem=send2.at[slot, k],
            recv_sem=recv2.at[slot, k],
            device_id={"stn": to, "chan": chan},
            device_id_type=MESH,
        )
        copy.start()
        sends.append(copy)

    def share(block, k):
        if k % KS < KS - 1:
            return
        copy = pltpu.make_async_remote_copy(
            src_ref=whole(block, k // KS),
            dst_ref=whole(block, k // KS),
            send_sem=sib_send.at[block, k // KS],
            recv_sem=sib_recv.at[block, k // KS],
            device_id={"stn": sibling, "chan": chan},
            device_id_type=MESH,
        )
        copy.start()
        sends.append(copy)

    def arrive(block, k):
        pltpu.make_async_remote_copy(
            src_ref=part(block, k),
            dst_ref=part(block, k),
            send_sem=send2.at[block, k],
            recv_sem=recv2.at[block, k],
            device_id={"stn": right, "chan": chan},
            device_id_type=MESH,
        ).wait_recv()

    for half in range(HALVES):

        @pl.loop(1, nchan)
        def _(step):
            turn(half, step).wait_recv()

        @pl.loop(0, RCAP)
        def _(r):
            block = arrived[half][source[r]]
            gathered[half, stn, r] = jnp.where(r < count, block, jnp.zeros_like(block))

        for k in range(half * KS, (half + 1) * KS):
            push(OWN, k, right, L0)
            push(OWN, k, left, R0)
            push(OWN, k, across, Y0)
            share(OWN, k)

    def far(k):
        arrive(F0, k)
        push(F0, k, across, F1)
        share(F0, k)

    for k in range(KCH):
        arrive(R0, k)
        if k % 2 == 0:
            push(R0, k, left, F0)
        arrive(L0, k)
        if k % 2 == 1:
            push(L0, k, right, F0)
        arrive(Y0, k)
        push(Y0, k, right, L1)
        push(Y0, k, left, R1)
        for block in (R0, L0, Y0):
            share(block, k)
        if k >= 2:
            far(k - 2)
    for k in range(KCH - 2, KCH):
        far(k)
    for k in range(KCH):
        arrive(R1, k)
        share(R1, k)
        arrive(L1, k)
        share(L1, k)
    for k in range(KCH):
        arrive(F1, k)
        share(F1, k)
    for block in range(8):
        for half in range(HALVES):
            pltpu.make_async_remote_copy(
                src_ref=whole(block, half, 1),
                dst_ref=whole(block, half, 1),
                send_sem=sib_send.at[block, half],
                recv_sem=sib_recv.at[block, half],
                device_id={"stn": sibling, "chan": chan},
                device_id_type=MESH,
            ).wait_recv()
    for half in range(HALVES):

        @pl.loop(1, nchan)
        def _(step):
            turn(half, step).wait_send()

    for copy in sends:
        copy.wait_send()


def front(volts, taps, survive, owner, stn_count):
    inputs = volts.shape[2]
    lanes = 2 * inputs
    nchan = owner.shape[1]
    dma = pltpu.SemaphoreType.DMA
    return pl.pallas_call(
        front_kernel,
        out_shape=jax.ShapeDtypeStruct((HALVES, stn_count, RCAP, HALF, lanes), BF16),
        in_specs=[
            pl.BlockSpec(memory_space=pltpu.SMEM),
            pl.BlockSpec(memory_space=pltpu.SMEM),
            pl.BlockSpec(memory_space=pltpu.VMEM),
            pl.BlockSpec(memory_space=pltpu.HBM),
        ],
        out_specs=pl.BlockSpec(memory_space=pltpu.VMEM),
        scratch_shapes=[
            pltpu.VMEM((2, inputs, NS * FINE), BF16),
            pltpu.VMEM((TAPS * 16, FINE), BF16),
            pltpu.VMEM((NS, TAPS * 16, lanes), F32),
            pltpu.VMEM((KEEP * HALF, lanes), F32),
            pltpu.VMEM((KEEP, HALF, lanes), BF16),
            pltpu.VMEM((HALVES, nchan * CAP, HALF, lanes), BF16),
            pltpu.VMEM((nchan * CAP, HALF, lanes), BF16),
            pltpu.VMEM((nchan * CAP, HALF, lanes), BF16),
            pltpu.SMEM((nchan * CAP,), jnp.int32),
            pltpu.SMEM((RCAP,), jnp.int32),
            dma((len(CHUNKS),)),
            dma((HALVES, nchan)),
            dma((HALVES, nchan)),
            dma((8, KCH)),
            dma((8, KCH)),
            dma((8, HALVES)),
            dma((8, HALVES)),
        ],
        compiler_params=pltpu.CompilerParams(
            collective_id=0, has_side_effects=True, vmem_limit_bytes=48 << 20
        ),
        name="front",
    )(survive, owner, taps, volts)


def correlate_kernel(stn_count, gathered, out_ref, built, sems):
    stn = lax.axis_index("stn")
    low = lax.broadcasted_iota(jnp.int32, (NSPEC, 128), 1) < 64

    def series(n, slot):
        return jnp.concatenate([gathered[h, n, slot] for h in range(HALVES)], 0).astype(F32)

    def store(slot):
        return pltpu.make_async_copy(built.at[slot], out_ref.at[0, slot], sems.at[slot])

    def correlate_slot(slot):
        own = series(stn, slot) * (1.0 / NSPEC)
        turned = swap_halves(own)
        turned = jnp.where(low, turned, -turned)
        left = jnp.concatenate([own, turned], 0).astype(BF16)
        for n in range(0, stn_count, 4):
            columns = []
            for m in range(n, n + 4, 2):
                first, second = series(m, slot), series(m + 1, slot)
                real = jnp.where(low, first, swap_halves(second))
                imag = jnp.where(low, swap_halves(first), second)
                columns.append(jnp.concatenate([real, imag], 0).astype(BF16))
            product = lax.dot_general(
                left,
                jnp.concatenate(columns, 1),
                (((0,), (0,)), ((), ())),
                preferred_element_type=F32,
            )
            built[slot, :, :, n * 64 : (n + 4) * 64] = product.astype(BF16).reshape(2, 64, 256)
        store(slot).start()

    @pl.loop(0, RCAP // SLOTS_STEP)
    def _(step):
        for u in range(SLOTS_STEP):
            correlate_slot(step * SLOTS_STEP + u)

    @pl.loop(0, RCAP)
    def _(slot):
        store(slot).wait()


def correlate(gathered):
    stn_count, lanes = gathered.shape[1], gathered.shape[4]
    inputs = lanes // 2
    return pl.pallas_call(
        functools.partial(correlate_kernel, stn_count),
        out_shape=jax.ShapeDtypeStruct((1, RCAP, 2, inputs, stn_count * inputs), BF16),
        in_specs=[pl.BlockSpec(memory_space=pltpu.VMEM)],
        out_specs=pl.BlockSpec(memory_space=pltpu.HBM),
        scratch_shapes=[
            pltpu.VMEM((RCAP, 2, inputs, stn_count * inputs), BF16),
            pltpu.SemaphoreType.DMA((RCAP,)),
        ],
        compiler_params=pltpu.CompilerParams(vmem_limit_bytes=16 << 20),
        name="correlate",
    )(gathered)


def per_device(volts, taps, survive, owner):
    volts, taps, survive, owner = [pltpu.with_memory_space_constraint(v, pltpu.HBM) for v in (volts, taps, survive.T, owner.T)]
    gathered = front(volts, taps, survive, owner, lax.axis_size("stn"))
    return correlate(gathered)


def solution(mesh):
    return jax.shard_map(
        per_device,
        mesh=mesh,
        in_specs=(P("chan", None, "stn", None), P(), P(), P()),
        out_specs=P("chan", None, None, "stn", None),
        check_vma=False,
    )
```

```python
import functools
import math

import jax
import jax.numpy as jnp
from jax import lax
from jax.experimental import pallas as pl
from jax.experimental.pallas import tpu as pltpu
from jax.sharding import PartitionSpec as P

RCAP = 24
CAP = 2
FINE = 384
TAPS = 16
NSPEC = 32
KEEP = 8
NS = NSPEC + TAPS - 1
F32 = jnp.float32
BF16 = jnp.bfloat16
MESH = pl.DeviceIdType.MESH


def swap_halves(x):
    return pltpu.roll(x, 64, 1)


def trig_tables(chosen, branch):
    product = chosen * branch
    turns = jnp.floor((product + 0.5) * (1.0 / FINE))
    phase = product - turns * FINE
    quarter = jnp.floor((phase + (FINE // 8)) * (4.0 / FINE) + 1e-4)
    angle = (phase - quarter * (FINE // 4)) * (2.0 * math.pi / FINE)
    square = angle * angle
    sine = angle * (
        1.0
        + square
        * (-1.0 / 6 + square * (1.0 / 120 + square * (-1.0 / 5040 + square * (1.0 / 362880))))
    )
    cosine = 1.0 + square * (
        -0.5
        + square
        * (1.0 / 24 + square * (-1.0 / 720 + square * (1.0 / 40320 - square * (1.0 / 3628800))))
    )
    odd = (quarter == 1.0) | (quarter == 3.0)
    c = jnp.where(odd, sine, cosine)
    s = jnp.where(odd, cosine, sine)
    c = jnp.where((quarter == 1.0) | (quarter == 2.0), -c, c)
    s = jnp.where((quarter == 2.0) | (quarter == 3.0), -s, s)
    factor = 1.0 / math.sqrt(FINE)
    return ((c * factor).astype(BF16).astype(F32), (s * factor).astype(BF16).astype(F32))


CHUNKS = ((0, 12), (12, 23), (23, 31), (31, 39), (39, NS))
SLOTS_STEP = 8
PARTS = 4
SPAN = NSPEC // PARTS
GROUPS = ((0, 1), (1, 2), (2, 4))
OWN, Y0, R0, L0, R1, L1, F0, F1 = range(8)
PLACES = {
    OWN: (0, 0), Y0: (0, 1), R0: (1, 0), L0: (3, 0), R1: (1, 1), L1: (3, 1), F0: (2, 0), F1: (2, 1)
}


def front_kernel(
    survive_hbm, owner_hbm, taps_hbm, volts_ref, gathered,
    survive_ref, owner_ref, taps_ref, buf, weights, partial, rows, channels, outbox, arrived0, arrived1, arrived2, pick, source,
    small_sem, load_sem, send1, recv1, send2, recv2, sib_send, sib_recv,
):
    arrived = (arrived0, arrived1, arrived2)
    stn = lax.axis_index("stn")
    chan = lax.axis_index("chan")
    nchan = lax.axis_size("chan")
    x, y, core = stn // 4, (stn // 2) % 2, stn % 2

    def name(dx, dy, dcore=0):
        return ((x + dx) % 4) * 4 + ((y + dy) % 2) * 2 + (core + dcore) % 2

    right, left, across, sibling = name(1, 0), name(3, 0), name(0, 1), name(0, 0, 1)

    def load(n):
        lanes = pl.ds(CHUNKS[n][0] * FINE, (CHUNKS[n][1] - CHUNKS[n][0]) * FINE)
        return pltpu.make_async_copy(
            volts_ref.at[0, :, :, lanes], buf.at[:, :, lanes], load_sem.at[n]
        )

    small = [
        pltpu.make_async_copy(source, target, small_sem.at[n])
        for n, (source, target) in enumerate(
            ((survive_hbm, survive_ref), (taps_hbm, taps_ref), (owner_hbm, owner_ref))
        )
    ]
    for copy in small:
        copy.start()
    for n in range(len(CHUNKS)):
        load(n).start()

    barrier = pltpu.get_barrier_semaphore()
    for other in (right, left, across, sibling):
        pl.semaphore_signal(
            barrier, inc=1, device_id={"stn": other, "chan": chan}, device_id_type=MESH
        )

    @pl.loop(1, nchan)
    def _(step):
        pl.semaphore_signal(
            barrier,
            inc=1,
            device_id={"stn": stn, "chan": (chan + step) % nchan},
            device_id_type=MESH,
        )

    for copy in small:
        copy.wait()

    row = lax.broadcasted_iota(jnp.int32, (KEEP, FINE), 0)
    branch = lax.broadcasted_iota(jnp.int32, (KEEP, FINE), 1).astype(F32)
    chosen = jnp.zeros((KEEP, FINE), jnp.int32)
    for j in range(KEEP):
        chosen = jnp.where(row == j, survive_ref[j, chan], chosen)
    cosine, sine = trig_tables(chosen.astype(F32), branch)
    both = jnp.concatenate([cosine, sine], 0)
    for p in range(TAPS):
        weights[p * 16 : (p + 1) * 16, :] = (both * taps_ref[p : p + 1, :]).astype(BF16)

    targets = []
    owners = [owner_ref[j, chan] for j in range(KEEP)]
    for j in range(KEEP):
        rank = jnp.int32(0)
        for other in range(j):
            rank = rank + (owners[other] == owners[j]).astype(jnp.int32)
        targets.append(owners[j] * CAP + rank)

    for slot in range(nchan * CAP):
        found = jnp.int32(0)
        for j in range(1, KEEP):
            found = jnp.where(targets[j] == slot, j, found)
        pick[slot] = found

    def transform(first, width):
        block = jnp.concatenate(
            [
                buf[:, :, (first + u) * FINE : (first + u + 1) * FINE].reshape(128, FINE)
                for u in range(width)
            ],
            0,
        )
        product = lax.dot_general(
            weights[...], block, (((1,), (1,)), ((), ())), preferred_element_type=F32
        )
        for u in range(width):
            partial[first + u] = product[:, u * 128 : (u + 1) * 128]

    def finish(t):
        total = partial[t, 0:16, :]
        for p in range(1, TAPS):
            total = total + partial[t + p, p * 16 : (p + 1) * 16, :]
        swapped = swap_halves(total[8:16])
        rows[pl.ds(t % SPAN, KEEP, stride=SPAN), :] = total[0:8] + jnp.where(
            lane < 64, swapped, -swapped
        )

    lane = lax.broadcasted_iota(jnp.int32, (KEEP, 128), 1)

    def turn(group, step):
        to = (chan + step) % nchan
        lo, hi = GROUPS[group]
        return pltpu.make_async_remote_copy(
            src_ref=outbox.at[lo:hi, pl.ds(to * CAP, CAP)],
            dst_ref=arrived[group].at[:, pl.ds(chan * CAP, CAP)],
            send_sem=send1.at[group, step],
            recv_sem=recv1.at[group, step],
            device_id={"stn": stn, "chan": to},
            device_id_type=MESH,
        )

    chunk = 0
    done = 0
    for group, (lo, hi) in enumerate(GROUPS):
        for q in range(lo, hi):
            while done < (q + 1) * SPAN:
                load(chunk).wait()
                begin, end = CHUNKS[chunk]
                chunk += 1
                for first in range(begin, end, 2):
                    width = min(2, end - first)
                    transform(first, width)
                    while done + TAPS <= first + width and done < (q + 1) * SPAN:
                        finish(done)
                        done += 1

            for j in range(KEEP):
                channels[j] = rows[j * SPAN : (j + 1) * SPAN, :].astype(BF16)
            for slot in range(nchan * CAP):
                outbox[q, slot] = channels[pick[slot]]

        if group == 0:
            pl.semaphore_wait(barrier, 4 + nchan - 1)

        @pl.loop(0, nchan - 1)
        def _(i):
            turn(group, nchan // 2 + ((i + 1) // 2) * (2 * (i % 2) - 1)).start()

        for q in range(lo, hi):
            mine = pl.ds(chan * CAP, CAP)
            arrived[group][q - lo, mine] = outbox[q, mine]

    counts = []
    count = jnp.int32(0)
    for b in range(nchan):
        for j in range(KEEP):
            count = count + (owner_ref[j, b] == chan).astype(jnp.int32)
        counts.append(count)

    @pl.loop(0, RCAP)
    def _(r):
        skip = jnp.int32(0)
        for b in range(nchan):
            skip = jnp.where(counts[b] <= r, (b + 1) * CAP - counts[b], skip)
        source[r] = jnp.minimum(r + skip, nchan * CAP - 1)

    sends = []

    def part(block, k):
        dx, dy = PLACES[block]
        return gathered.at[k, name(dx, dy)]

    def two(block, half, dcore=0):
        dx, dy = PLACES[block]
        return gathered.at[2 * half : 2 * half + 2, name(dx, dy, dcore)]

    def push(block, k, to, slot):
        copy = pltpu.make_async_remote_copy(
            src_ref=part(block, k),
            dst_ref=part(block, k),
            send_sem=send2.at[slot, k],
            recv_sem=recv2.at[slot, k],
            device_id={"stn": to, "chan": chan},
            device_id_type=MESH,
        )
        copy.start()
        sends.append(copy)

    def share(block, half):
        copy = pltpu.make_async_remote_copy(
            src_ref=two(block, half),
            dst_ref=two(block, half),
            send_sem=sib_send.at[block, half],
            recv_sem=sib_recv.at[block, half],
            device_id={"stn": sibling, "chan": chan},
            device_id_type=MESH,
        )
        copy.start()
        sends.append(copy)

    def from_sibling(block, half):
        pltpu.make_async_remote_copy(
            src_ref=two(block, half, 1),
            dst_ref=two(block, half, 1),
            send_sem=sib_send.at[block, half],
            recv_sem=sib_recv.at[block, half],
            device_id={"stn": sibling, "chan": chan},
            device_id_type=MESH,
        ).wait_recv()

    def arrive(block, k):
        pltpu.make_async_remote_copy(
            src_ref=part(block, k),
            dst_ref=part(block, k),
            send_sem=send2.at[block, k],
            recv_sem=recv2.at[block, k],
            device_id={"stn": right, "chan": chan},
            device_id_type=MESH,
        ).wait_recv()

    def own(group):
        @pl.loop(1, nchan)
        def _(step):
            turn(group, step).wait_recv()

        lo, hi = GROUPS[group]
        for k in range(lo, hi):

            @pl.loop(0, RCAP, unroll=4)
            def _(r):
                block = arrived[group][k - lo, source[r]]
                gathered[k, stn, r] = jnp.where(r < count, block, jnp.zeros_like(block))

            push(OWN, k, right, L0)
            push(OWN, k, left, R0)
            push(OWN, k, across, Y0)

    def beside(k):
        if k % 2 == 0:
            arrive(R0, k)
            push(R0, k, left, F0)
            arrive(L0, k)
        else:
            arrive(L0, k)
            push(L0, k, right, F0)
            arrive(R0, k)

    def pair(k):
        arrive(Y0, k)
        push(Y0, k, right, L1)
        push(Y0, k, left, R1)

    def far(k):
        arrive(F0, k)
        push(F0, k, across, F1)

    own(0)
    own(1)
    share(OWN, 0)
    beside(0)
    pair(0)
    own(2)
    beside(1)
    pair(1)
    share(OWN, 1)
    far(0)
    for block in (R0, L0, Y0):
        share(block, 0)
    beside(2)
    beside(3)
    pair(2)
    pair(3)
    far(1)
    for group in range(len(GROUPS)):

        @pl.loop(1, nchan)
        def _(step):
            turn(group, step).wait_send()

    share(R0, 1)
    share(L0, 1)
    share(Y0, 1)
    share(F0, 0)
    early = len(sends)
    far(2)
    far(3)
    share(F0, 1)
    for block in (R1, L1, F1):
        arrive(block, 0)
        arrive(block, 1)
        share(block, 0)
    for copy in sends[:early]:
        copy.wait_send()
    for half in range(2):
        for block in (OWN, R0, L0, Y0):
            from_sibling(block, half)
    for block in (R1, L1):
        arrive(block, 2)
    arrive(R1, 3)
    share(R1, 1)
    arrive(L1, 3)
    share(L1, 1)
    arrive(F1, 2)
    arrive(F1, 3)
    share(F1, 1)
    for half in range(2):
        for block in (F0, R1, L1, F1):
            from_sibling(block, half)
    for copy in sends[early:]:
        copy.wait_send()


def front(volts, taps, survive, owner, stn_count):
    inputs = volts.shape[2]
    lanes = 2 * inputs
    nchan = owner.shape[1]
    dma = pltpu.SemaphoreType.DMA
    return pl.pallas_call(
        front_kernel,
        out_shape=jax.ShapeDtypeStruct((PARTS, stn_count, RCAP, SPAN, lanes), BF16),
        in_specs=[pl.BlockSpec(memory_space=pltpu.HBM)] * 4,
        out_specs=pl.BlockSpec(memory_space=pltpu.VMEM),
        scratch_shapes=[
            pltpu.SMEM(survive.shape, jnp.int32),
            pltpu.SMEM(owner.shape, jnp.int32),
            pltpu.VMEM(taps.shape, F32),
            pltpu.VMEM((2, inputs, NS * FINE), BF16),
            pltpu.VMEM((TAPS * 16, FINE), BF16),
            pltpu.VMEM((NS, TAPS * 16, lanes), F32),
            pltpu.VMEM((KEEP * SPAN, lanes), F32),
            pltpu.VMEM((KEEP, SPAN, lanes), BF16),
            pltpu.VMEM((PARTS, nchan * CAP, SPAN, lanes), BF16),
            *[pltpu.VMEM((hi - lo, nchan * CAP, SPAN, lanes), BF16) for lo, hi in GROUPS],
            pltpu.SMEM((nchan * CAP,), jnp.int32),
            pltpu.SMEM((RCAP,), jnp.int32),
            dma((3,)),
            dma((len(CHUNKS),)),
            dma((len(GROUPS), nchan)),
            dma((len(GROUPS), nchan)),
            dma((8, PARTS)),
            dma((8, PARTS)),
            dma((8, 2)),
            dma((8, 2)),
        ],
        compiler_params=pltpu.CompilerParams(
            collective_id=0, has_side_effects=True, vmem_limit_bytes=48 << 20
        ),
        name="front",
    )(survive, owner, taps, volts)


def correlate_kernel(stn_count, gathered, out_ref, built, sems):
    stn = lax.axis_index("stn")
    low = lax.broadcasted_iota(jnp.int32, (NSPEC, 128), 1) < 64

    def series(n, slot):
        return jnp.concatenate([gathered[k, n, slot].astype(F32) for k in range(PARTS)], 0)

    def store(slot):
        return pltpu.make_async_copy(built.at[slot], out_ref.at[0, slot], sems.at[slot])

    def correlate_slot(slot):
        own = series(stn, slot) * (1.0 / NSPEC)
        turned = swap_halves(own)
        turned = jnp.where(low, turned, -turned)
        left = jnp.concatenate([own, turned], 0).astype(BF16)
        for n in range(0, stn_count, 4):
            columns = []
            for m in range(n, n + 4, 2):
                first, second = series(m, slot), series(m + 1, slot)
                real = jnp.where(low, first, swap_halves(second))
                imag = jnp.where(low, swap_halves(first), second)
                columns.append(jnp.concatenate([real, imag], 0).astype(BF16))
            product = lax.dot_general(
                left,
                jnp.concatenate(columns, 1),
                (((0,), (0,)), ((), ())),
                preferred_element_type=F32,
            )
            built[slot, :, :, n * 64 : (n + 4) * 64] = product.astype(BF16).reshape(2, 64, 256)
        store(slot).start()

    @pl.loop(0, RCAP // SLOTS_STEP)
    def _(step):
        for u in range(SLOTS_STEP):
            correlate_slot(step * SLOTS_STEP + u)

    @pl.loop(0, RCAP)
    def _(slot):
        store(slot).wait()


def correlate(gathered):
    stn_count, lanes = gathered.shape[1], gathered.shape[4]
    inputs = lanes // 2
    return pl.pallas_call(
        functools.partial(correlate_kernel, stn_count),
        out_shape=jax.ShapeDtypeStruct((1, RCAP, 2, inputs, stn_count * inputs), BF16),
        in_specs=[pl.BlockSpec(memory_space=pltpu.VMEM)],
        out_specs=pl.BlockSpec(memory_space=pltpu.HBM),
        scratch_shapes=[
            pltpu.VMEM((RCAP, 2, inputs, stn_count * inputs), BF16),
            pltpu.SemaphoreType.DMA((RCAP,)),
        ],
        compiler_params=pltpu.CompilerParams(vmem_limit_bytes=16 << 20),
        name="correlate",
    )(gathered)


def per_device(volts, taps, survive, owner):
    volts, taps, survive, owner = [pltpu.with_memory_space_constraint(v, pltpu.HBM) for v in (volts, taps, survive.T, owner.T)]
    gathered = front(volts, taps, survive, owner, lax.axis_size("stn"))
    return correlate(gathered)


def solution(mesh):
    return jax.shard_map(
        per_device,
        mesh=mesh,
        in_specs=(P("chan", None, "stn", None), P(), P(), P()),
        out_specs=P("chan", None, None, "stn", None),
        check_vma=False,
    )
```

```python
import functools
import math

import jax
import jax.numpy as jnp
from jax import lax
from jax.experimental import pallas as pl
from jax.experimental.pallas import tpu as pltpu
from jax.sharding import PartitionSpec as P

RCAP = 24
CAP = 2
FINE = 384
TAPS = 16
NSPEC = 32
KEEP = 8
NS = NSPEC + TAPS - 1
F32 = jnp.float32
BF16 = jnp.bfloat16
MESH = pl.DeviceIdType.MESH


def swap_halves(x):
    return pltpu.roll(x, 64, 1)


def trig_tables(chosen, branch):
    product = chosen * branch
    turns = jnp.floor((product + 0.5) * (1.0 / FINE))
    phase = product - turns * FINE
    quarter = jnp.floor((phase + (FINE // 8)) * (4.0 / FINE) + 1e-4)
    angle = (phase - quarter * (FINE // 4)) * (2.0 * math.pi / FINE)
    square = angle * angle
    sine = angle * (
        1.0
        + square
        * (-1.0 / 6 + square * (1.0 / 120 + square * (-1.0 / 5040 + square * (1.0 / 362880))))
    )
    cosine = 1.0 + square * (
        -0.5
        + square
        * (1.0 / 24 + square * (-1.0 / 720 + square * (1.0 / 40320 - square * (1.0 / 3628800))))
    )
    odd = (quarter == 1.0) | (quarter == 3.0)
    c = jnp.where(odd, sine, cosine)
    s = jnp.where(odd, cosine, sine)
    c = jnp.where((quarter == 1.0) | (quarter == 2.0), -c, c)
    s = jnp.where((quarter == 2.0) | (quarter == 3.0), -s, s)
    factor = 1.0 / math.sqrt(FINE)
    return ((c * factor).astype(BF16).astype(F32), (s * factor).astype(BF16).astype(F32))


CHUNKS = ((0, 12), (12, 23), (23, 31), (31, 39), (39, NS))
SLOTS_STEP = 8
PARTS = 4
SPAN = NSPEC // PARTS
GROUPS = ((0, 2), (2, 4))
OWN, Y0, R0, L0, R1, L1, F0, F1 = range(8)
PLACES = {
    OWN: (0, 0), Y0: (0, 1), R0: (1, 0), L0: (3, 0), R1: (1, 1), L1: (3, 1), F0: (2, 0), F1: (2, 1)
}


def front_kernel(
    survive_hbm, owner_hbm, taps_hbm, volts_ref, gathered,
    survive_ref, owner_ref, taps_ref, buf, weights, partial, rows, channels, outbox, arrived0, arrived1, pick, source,
    small_sem, load_sem, send1, recv1, send2, recv2, sib_send, sib_recv,
):
    arrived = (arrived0, arrived1)
    stn = lax.axis_index("stn")
    chan = lax.axis_index("chan")
    nchan = lax.axis_size("chan")
    x, y, core = lax.div(stn, 4), lax.rem(lax.div(stn, 2), 2), lax.rem(stn, 2)
    names = {
        (dx, dy, dcore): lax.rem(x + dx, 4) * 4 + lax.rem(y + dy, 2) * 2 + lax.rem(core + dcore, 2)
        for dx in range(4)
        for dy in range(2)
        for dcore in range(2)
    }

    def name(dx, dy, dcore=0):
        return names[dx, dy, dcore]

    right, left, across, sibling = name(1, 0), name(3, 0), name(0, 1), name(0, 0, 1)

    def load(n):
        lanes = pl.ds(CHUNKS[n][0] * FINE, (CHUNKS[n][1] - CHUNKS[n][0]) * FINE)
        return pltpu.make_async_copy(
            volts_ref.at[0, :, :, lanes], buf.at[:, :, lanes], load_sem.at[n]
        )

    small = [
        pltpu.make_async_copy(source, target, small_sem.at[n])
        for n, (source, target) in enumerate(
            ((survive_hbm, survive_ref), (taps_hbm, taps_ref), (owner_hbm, owner_ref))
        )
    ]
    for copy in small:
        copy.start()
    for n in range(len(CHUNKS)):
        load(n).start()

    barrier = pltpu.get_barrier_semaphore()
    for other in (right, left, across, sibling):
        pl.semaphore_signal(
            barrier, inc=1, device_id={"stn": other, "chan": chan}, device_id_type=MESH
        )

    @pl.loop(1, nchan)
    def _(step):
        pl.semaphore_signal(
            barrier,
            inc=1,
            device_id={"stn": stn, "chan": (chan + step) % nchan},
            device_id_type=MESH,
        )

    for copy in small:
        copy.wait()

    row = lax.broadcasted_iota(jnp.int32, (KEEP, FINE), 0)
    branch = lax.broadcasted_iota(jnp.int32, (KEEP, FINE), 1).astype(F32)
    chosen = jnp.zeros((KEEP, FINE), jnp.int32)
    for j in range(KEEP):
        chosen = jnp.where(row == j, survive_ref[j, chan], chosen)
    cosine, sine = trig_tables(chosen.astype(F32), branch)
    both = jnp.concatenate([cosine, sine], 0)
    for p in range(TAPS):
        weights[p * 16 : (p + 1) * 16, :] = (both * taps_ref[p : p + 1, :]).astype(BF16)

    targets = []
    owners = [owner_ref[j, chan] for j in range(KEEP)]
    for j in range(KEEP):
        rank = jnp.int32(0)
        for other in range(j):
            rank = rank + (owners[other] == owners[j]).astype(jnp.int32)
        targets.append(owners[j] * CAP + rank)

    for slot in range(nchan * CAP):
        found = jnp.int32(0)
        for j in range(1, KEEP):
            found = jnp.where(targets[j] == slot, j, found)
        pick[slot] = found

    def transform(first, width):
        block = jnp.concatenate(
            [
                buf[:, :, (first + u) * FINE : (first + u + 1) * FINE].reshape(128, FINE)
                for u in range(width)
            ],
            0,
        )
        product = lax.dot_general(
            weights[...], block, (((1,), (1,)), ((), ())), preferred_element_type=F32
        )
        for u in range(width):
            partial[first + u] = product[:, u * 128 : (u + 1) * 128]

    def finish(t):
        total = partial[t, 0:16, :]
        for p in range(1, TAPS):
            total = total + partial[t + p, p * 16 : (p + 1) * 16, :]
        swapped = swap_halves(total[8:16])
        rows[pl.ds(t % SPAN, KEEP, stride=SPAN), :] = total[0:8] + jnp.where(
            lane < 64, swapped, -swapped
        )

    lane = lax.broadcasted_iota(jnp.int32, (KEEP, 128), 1)

    def turn(group, step):
        to = lax.rem(chan + step, nchan)
        lo, hi = GROUPS[group]
        return pltpu.make_async_remote_copy(
            src_ref=outbox.at[lo:hi, pl.ds(to * CAP, CAP)],
            dst_ref=arrived[group].at[:, pl.ds(chan * CAP, CAP)],
            send_sem=send1.at[group, step],
            recv_sem=recv1.at[group, step],
            device_id={"stn": stn, "chan": to},
            device_id_type=MESH,
        )

    chunk = 0
    done = 0
    for group, (lo, hi) in enumerate(GROUPS):
        for q in range(lo, hi):
            while done < (q + 1) * SPAN:
                load(chunk).wait()
                begin, end = CHUNKS[chunk]
                chunk += 1
                for first in range(begin, end, 2):
                    width = min(2, end - first)
                    transform(first, width)
                    while done + TAPS <= first + width and done < (q + 1) * SPAN:
                        finish(done)
                        done += 1

            for j in range(KEEP):
                channels[j] = rows[j * SPAN : (j + 1) * SPAN, :].astype(BF16)
            for slot in range(nchan * CAP):
                outbox[q, slot] = channels[pick[slot]]

        if group == 0:
            pl.semaphore_wait(barrier, 4 + nchan - 1)

        for i in range(nchan - 1):
            turn(group, nchan // 2 + ((i + 1) // 2) * (2 * (i % 2) - 1)).start()

        for q in range(lo, hi):
            mine = pl.ds(chan * CAP, CAP)
            arrived[group][q - lo, mine] = outbox[q, mine]

    counts = []
    count = jnp.int32(0)
    for b in range(nchan):
        for j in range(KEEP):
            count = count + (owner_ref[j, b] == chan).astype(jnp.int32)
        counts.append(count)

    @pl.loop(0, RCAP)
    def _(r):
        skip = jnp.int32(0)
        for b in range(nchan):
            skip = jnp.where(counts[b] <= r, (b + 1) * CAP - counts[b], skip)
        source[r] = jnp.minimum(r + skip, nchan * CAP - 1)

    sends = []

    def part(block, k):
        dx, dy = PLACES[block]
        return gathered.at[k, name(dx, dy)]

    def two(block, half, dcore=0):
        dx, dy = PLACES[block]
        return gathered.at[2 * half : 2 * half + 2, name(dx, dy, dcore)]

    def push(block, k, to, slot):
        copy = pltpu.make_async_remote_copy(
            src_ref=part(block, k),
            dst_ref=part(block, k),
            send_sem=send2.at[slot, k],
            recv_sem=recv2.at[slot, k],
            device_id={"stn": to, "chan": chan},
            device_id_type=MESH,
        )
        copy.start()
        sends.append(copy)

    def share(block, half):
        copy = pltpu.make_async_remote_copy(
            src_ref=two(block, half),
            dst_ref=two(block, half),
            send_sem=sib_send.at[block, half],
            recv_sem=sib_recv.at[block, half],
            device_id={"stn": sibling, "chan": chan},
            device_id_type=MESH,
        )
        copy.start()
        sends.append(copy)

    def from_sibling(block, half):
        pltpu.make_async_remote_copy(
            src_ref=two(block, half, 1),
            dst_ref=two(block, half, 1),
            send_sem=sib_send.at[block, half],
            recv_sem=sib_recv.at[block, half],
            device_id={"stn": sibling, "chan": chan},
            device_id_type=MESH,
        ).wait_recv()

    def arrive(block, k):
        pltpu.make_async_remote_copy(
            src_ref=part(block, k),
            dst_ref=part(block, k),
            send_sem=send2.at[block, k],
            recv_sem=recv2.at[block, k],
            device_id={"stn": right, "chan": chan},
            device_id_type=MESH,
        ).wait_recv()

    def own(group):
        @pl.loop(1, nchan)
        def _(step):
            turn(group, step).wait_recv()

        lo, hi = GROUPS[group]
        for k in range(lo, hi):

            @pl.loop(0, RCAP, unroll=4)
            def _(r):
                block = arrived[group][k - lo, source[r]]
                gathered[k, stn, r] = jnp.where(r < count, block, jnp.zeros_like(block))

            push(OWN, k, right, L0)
            push(OWN, k, left, R0)
            push(OWN, k, across, Y0)

    def beside(k):
        if k % 2 == 0:
            arrive(R0, k)
            push(R0, k, left, F0)
            arrive(L0, k)
        else:
            arrive(L0, k)
            push(L0, k, right, F0)
            arrive(R0, k)

    def pair(k):
        arrive(Y0, k)
        push(Y0, k, right, L1)
        push(Y0, k, left, R1)

    def far(k):
        arrive(F0, k)
        push(F0, k, across, F1)

    own(0)
    share(OWN, 0)
    own(1)
    beside(0)
    beside(1)
    pair(0)
    pair(1)
    share(OWN, 1)
    far(0)
    for block in (R0, L0, Y0):
        share(block, 0)
    beside(2)
    beside(3)
    pair(2)
    pair(3)
    far(1)
    for group in range(len(GROUPS)):

        @pl.loop(1, nchan)
        def _(step):
            turn(group, step).wait_send()

    share(R0, 1)
    share(L0, 1)
    share(Y0, 1)
    share(F0, 0)
    early = len(sends)
    far(2)
    far(3)
    share(F0, 1)
    for block in (R1, L1, F1):
        arrive(block, 0)
        arrive(block, 1)
        share(block, 0)
    for copy in sends[:early]:
        copy.wait_send()
    for half in range(2):
        for block in (OWN, R0, L0, Y0):
            from_sibling(block, half)
    for block in (R1, L1):
        arrive(block, 2)
    arrive(R1, 3)
    share(R1, 1)
    arrive(L1, 3)
    share(L1, 1)
    arrive(F1, 2)
    arrive(F1, 3)
    share(F1, 1)
    for half in range(2):
        for block in (F0, R1, L1, F1):
            from_sibling(block, half)
    for copy in sends[early:]:
        copy.wait_send()


def front(volts, taps, survive, owner, stn_count):
    inputs = volts.shape[2]
    lanes = 2 * inputs
    nchan = owner.shape[1]
    dma = pltpu.SemaphoreType.DMA
    return pl.pallas_call(
        front_kernel,
        out_shape=jax.ShapeDtypeStruct((PARTS, stn_count, RCAP, SPAN, lanes), BF16),
        in_specs=[pl.BlockSpec(memory_space=pltpu.HBM)] * 4,
        out_specs=pl.BlockSpec(memory_space=pltpu.VMEM),
        scratch_shapes=[
            pltpu.SMEM(survive.shape, jnp.int32),
            pltpu.SMEM(owner.shape, jnp.int32),
            pltpu.VMEM(taps.shape, F32),
            pltpu.VMEM((2, inputs, NS * FINE), BF16),
            pltpu.VMEM((TAPS * 16, FINE), BF16),
            pltpu.VMEM((NS, TAPS * 16, lanes), F32),
            pltpu.VMEM((KEEP * SPAN, lanes), F32),
            pltpu.VMEM((KEEP, SPAN, lanes), BF16),
            pltpu.VMEM((PARTS, nchan * CAP, SPAN, lanes), BF16),
            *[pltpu.VMEM((hi - lo, nchan * CAP, SPAN, lanes), BF16) for lo, hi in GROUPS],
            pltpu.SMEM((nchan * CAP,), jnp.int32),
            pltpu.SMEM((RCAP,), jnp.int32),
            dma((3,)),
            dma((len(CHUNKS),)),
            dma((len(GROUPS), nchan)),
            dma((len(GROUPS), nchan)),
            dma((8, PARTS)),
            dma((8, PARTS)),
            dma((8, 2)),
            dma((8, 2)),
        ],
        compiler_params=pltpu.CompilerParams(
            collective_id=0, has_side_effects=True, vmem_limit_bytes=48 << 20
        ),
        name="front",
    )(survive, owner, taps, volts)


def correlate_kernel(stn_count, gathered, out_ref, built, sems):
    stn = lax.axis_index("stn")
    low = lax.broadcasted_iota(jnp.int32, (NSPEC, 128), 1) < 64

    def series(n, slot):
        return jnp.concatenate([gathered[k, n, slot].astype(F32) for k in range(PARTS)], 0)

    def store(slot):
        return pltpu.make_async_copy(built.at[slot], out_ref.at[0, slot], sems.at[slot])

    def correlate_slot(slot):
        own = series(stn, slot) * (1.0 / NSPEC)
        turned = swap_halves(own)
        turned = jnp.where(low, turned, -turned)
        left = jnp.concatenate([own, turned], 0).astype(BF16)
        for n in range(0, stn_count, 4):
            columns = []
            for m in range(n, n + 4, 2):
                first, second = series(m, slot), series(m + 1, slot)
                real = jnp.where(low, first, swap_halves(second))
                imag = jnp.where(low, swap_halves(first), second)
                columns.append(jnp.concatenate([real, imag], 0).astype(BF16))
            product = lax.dot_general(
                left,
                jnp.concatenate(columns, 1),
                (((0,), (0,)), ((), ())),
                preferred_element_type=F32,
            )
            built[slot, :, :, n * 64 : (n + 4) * 64] = product.astype(BF16).reshape(2, 64, 256)
        store(slot).start()

    @pl.loop(0, RCAP // SLOTS_STEP)
    def _(step):
        for u in range(SLOTS_STEP):
            correlate_slot(step * SLOTS_STEP + u)

    @pl.loop(0, RCAP)
    def _(slot):
        store(slot).wait()


def correlate(gathered):
    stn_count, lanes = gathered.shape[1], gathered.shape[4]
    inputs = lanes // 2
    return pl.pallas_call(
        functools.partial(correlate_kernel, stn_count),
        out_shape=jax.ShapeDtypeStruct((1, RCAP, 2, inputs, stn_count * inputs), BF16),
        in_specs=[pl.BlockSpec(memory_space=pltpu.VMEM)],
        out_specs=pl.BlockSpec(memory_space=pltpu.HBM),
        scratch_shapes=[
            pltpu.VMEM((RCAP, 2, inputs, stn_count * inputs), BF16),
            pltpu.SemaphoreType.DMA((RCAP,)),
        ],
        compiler_params=pltpu.CompilerParams(vmem_limit_bytes=16 << 20),
        name="correlate",
    )(gathered)


def per_device(volts, taps, survive, owner):
    volts, taps, survive, owner = [pltpu.with_memory_space_constraint(v, pltpu.HBM) for v in (volts, taps, survive.T, owner.T)]
    gathered = front(volts, taps, survive, owner, lax.axis_size("stn"))
    return correlate(gathered)


def solution(mesh):
    return jax.shard_map(
        per_device,
        mesh=mesh,
        in_specs=(P("chan", None, "stn", None), P(), P(), P()),
        out_specs=P("chan", None, None, "stn", None),
        check_vma=False,
    )
```

```python
import functools
import math

import jax
import jax.numpy as jnp
from jax import lax
from jax.experimental import pallas as pl
from jax.experimental.pallas import tpu as pltpu
from jax.sharding import PartitionSpec as P

RCAP = 24
CAP = 2
FINE = 384
TAPS = 16
NSPEC = 32
KEEP = 8
NS = NSPEC + TAPS - 1
F32 = jnp.float32
BF16 = jnp.bfloat16
MESH = pl.DeviceIdType.MESH


def swap_halves(x):
    return pltpu.roll(x, 64, 1)


def trig_tables(chosen, branch):
    product = chosen * branch
    turns = jnp.floor((product + 0.5) * (1.0 / FINE))
    phase = product - turns * FINE
    quarter = jnp.floor((phase + (FINE // 8)) * (4.0 / FINE) + 1e-4)
    angle = (phase - quarter * (FINE // 4)) * (2.0 * math.pi / FINE)
    square = angle * angle
    sine = angle * (
        1.0
        + square
        * (-1.0 / 6 + square * (1.0 / 120 + square * (-1.0 / 5040 + square * (1.0 / 362880))))
    )
    cosine = 1.0 + square * (
        -0.5
        + square
        * (1.0 / 24 + square * (-1.0 / 720 + square * (1.0 / 40320 - square * (1.0 / 3628800))))
    )
    odd = (quarter == 1.0) | (quarter == 3.0)
    c = jnp.where(odd, sine, cosine)
    s = jnp.where(odd, cosine, sine)
    c = jnp.where((quarter == 1.0) | (quarter == 2.0), -c, c)
    s = jnp.where((quarter == 2.0) | (quarter == 3.0), -s, s)
    factor = 1.0 / math.sqrt(FINE)
    return ((c * factor).astype(BF16).astype(F32), (s * factor).astype(BF16).astype(F32))


CHUNKS = ((0, 12), (12, 23), (23, 31), (31, 39), (39, NS))
SLOTS_STEP = 8
PARTS = 4
SPAN = NSPEC // PARTS
GROUPS = ((0, 1), (1, 2), (2, 3), (3, 4))
OWN, Y0, R0, L0, R1, L1, F0, F1 = range(8)
PLACES = {
    OWN: (0, 0), Y0: (0, 1), R0: (1, 0), L0: (3, 0), R1: (1, 1), L1: (3, 1), F0: (2, 0), F1: (2, 1)
}


def front_kernel(
    survive_hbm, owner_hbm, taps_hbm, volts_ref, gathered,
    survive_ref, owner_ref, taps_ref, buf, weights, partial, rows, channels, outbox, arrived0, arrived1, arrived2, arrived3, pick, source,
    small_sem, load_sem, send1, recv1, send2, recv2, sib_send, sib_recv,
):
    arrived = (arrived0, arrived1, arrived2, arrived3)
    stn = lax.axis_index("stn")
    chan = lax.axis_index("chan")
    nchan = lax.axis_size("chan")
    x, y, core = stn // 4, (stn // 2) % 2, stn % 2

    def name(dx, dy, dcore=0):
        return ((x + dx) % 4) * 4 + ((y + dy) % 2) * 2 + (core + dcore) % 2

    right, left, across, sibling = name(1, 0), name(3, 0), name(0, 1), name(0, 0, 1)

    def load(n):
        lanes = pl.ds(CHUNKS[n][0] * FINE, (CHUNKS[n][1] - CHUNKS[n][0]) * FINE)
        return pltpu.make_async_copy(
            volts_ref.at[0, :, :, lanes], buf.at[:, :, lanes], load_sem.at[n]
        )

    small = [
        pltpu.make_async_copy(source, target, small_sem.at[n])
        for n, (source, target) in enumerate(
            ((survive_hbm, survive_ref), (taps_hbm, taps_ref), (owner_hbm, owner_ref))
        )
    ]
    for copy in small:
        copy.start()
    for n in range(len(CHUNKS)):
        load(n).start()

    barrier = pltpu.get_barrier_semaphore()
    for other in (right, left, across, sibling):
        pl.semaphore_signal(
            barrier, inc=1, device_id={"stn": other, "chan": chan}, device_id_type=MESH
        )

    @pl.loop(1, nchan)
    def _(step):
        pl.semaphore_signal(
            barrier,
            inc=1,
            device_id={"stn": stn, "chan": (chan + step) % nchan},
            device_id_type=MESH,
        )

    for copy in small:
        copy.wait()

    row = lax.broadcasted_iota(jnp.int32, (KEEP, FINE), 0)
    branch = lax.broadcasted_iota(jnp.int32, (KEEP, FINE), 1).astype(F32)
    chosen = jnp.zeros((KEEP, FINE), jnp.int32)
    for j in range(KEEP):
        chosen = jnp.where(row == j, survive_ref[j, chan], chosen)
    cosine, sine = trig_tables(chosen.astype(F32), branch)
    both = jnp.concatenate([cosine, sine], 0)
    for p in range(TAPS):
        weights[p * 16 : (p + 1) * 16, :] = (both * taps_ref[p : p + 1, :]).astype(BF16)

    targets = []
    owners = [owner_ref[j, chan] for j in range(KEEP)]
    for j in range(KEEP):
        rank = jnp.int32(0)
        for other in range(j):
            rank = rank + (owners[other] == owners[j]).astype(jnp.int32)
        targets.append(owners[j] * CAP + rank)

    for slot in range(nchan * CAP):
        found = jnp.int32(0)
        for j in range(1, KEEP):
            found = jnp.where(targets[j] == slot, j, found)
        pick[slot] = found

    def transform(first, width):
        block = jnp.concatenate(
            [
                buf[:, :, (first + u) * FINE : (first + u + 1) * FINE].reshape(128, FINE)
                for u in range(width)
            ],
            0,
        )
        product = lax.dot_general(
            weights[...], block, (((1,), (1,)), ((), ())), preferred_element_type=F32
        )
        for u in range(width):
            partial[first + u] = product[:, u * 128 : (u + 1) * 128]

    def finish(t):
        total = partial[t, 0:16, :]
        for p in range(1, TAPS):
            total = total + partial[t + p, p * 16 : (p + 1) * 16, :]
        swapped = swap_halves(total[8:16])
        rows[pl.ds(t % SPAN, KEEP, stride=SPAN), :] = total[0:8] + jnp.where(
            lane < 64, swapped, -swapped
        )

    lane = lax.broadcasted_iota(jnp.int32, (KEEP, 128), 1)

    def turn(group, step):
        to = (chan + step) % nchan
        lo, hi = GROUPS[group]
        return pltpu.make_async_remote_copy(
            src_ref=outbox.at[lo:hi, pl.ds(to * CAP, CAP)],
            dst_ref=arrived[group].at[:, pl.ds(chan * CAP, CAP)],
            send_sem=send1.at[group, step],
            recv_sem=recv1.at[group, step],
            device_id={"stn": stn, "chan": to},
            device_id_type=MESH,
        )

    chunk = 0
    done = 0
    for group, (lo, hi) in enumerate(GROUPS):
        for q in range(lo, hi):
            while done < (q + 1) * SPAN:
                load(chunk).wait()
                begin, end = CHUNKS[chunk]
                chunk += 1
                for first in range(begin, end, 2):
                    width = min(2, end - first)
                    transform(first, width)
                    while done + TAPS <= first + width and done < (q + 1) * SPAN:
                        finish(done)
                        done += 1

            for j in range(KEEP):
                channels[j] = rows[j * SPAN : (j + 1) * SPAN, :].astype(BF16)
            for slot in range(nchan * CAP):
                outbox[q, slot] = channels[pick[slot]]

        if group == 0:
            pl.semaphore_wait(barrier, 4 + nchan - 1)

        @pl.loop(0, nchan - 1)
        def _(i):
            turn(group, nchan // 2 + ((i + 1) // 2) * (2 * (i % 2) - 1)).start()

        for q in range(lo, hi):
            mine = pl.ds(chan * CAP, CAP)
            arrived[group][q - lo, mine] = outbox[q, mine]

    counts = []
    count = jnp.int32(0)
    for b in range(nchan):
        for j in range(KEEP):
            count = count + (owner_ref[j, b] == chan).astype(jnp.int32)
        counts.append(count)

    @pl.loop(0, RCAP)
    def _(r):
        skip = jnp.int32(0)
        for b in range(nchan):
            skip = jnp.where(counts[b] <= r, (b + 1) * CAP - counts[b], skip)
        source[r] = jnp.minimum(r + skip, nchan * CAP - 1)

    sends = []

    def part(block, k):
        dx, dy = PLACES[block]
        return gathered.at[k, name(dx, dy)]

    def two(block, half, dcore=0):
        dx, dy = PLACES[block]
        return gathered.at[2 * half : 2 * half + 2, name(dx, dy, dcore)]

    def push(block, k, to, slot):
        copy = pltpu.make_async_remote_copy(
            src_ref=part(block, k),
            dst_ref=part(block, k),
            send_sem=send2.at[slot, k],
            recv_sem=recv2.at[slot, k],
            device_id={"stn": to, "chan": chan},
            device_id_type=MESH,
        )
        copy.start()
        sends.append(copy)

    def share(block, half):
        copy = pltpu.make_async_remote_copy(
            src_ref=two(block, half),
            dst_ref=two(block, half),
            send_sem=sib_send.at[block, half],
            recv_sem=sib_recv.at[block, half],
            device_id={"stn": sibling, "chan": chan},
            device_id_type=MESH,
        )
        copy.start()
        sends.append(copy)

    def from_sibling(block, half):
        pltpu.make_async_remote_copy(
            src_ref=two(block, half, 1),
            dst_ref=two(block, half, 1),
            send_sem=sib_send.at[block, half],
            recv_sem=sib_recv.at[block, half],
            device_id={"stn": sibling, "chan": chan},
            device_id_type=MESH,
        ).wait_recv()

    def arrive(block, k):
        pltpu.make_async_remote_copy(
            src_ref=part(block, k),
            dst_ref=part(block, k),
            send_sem=send2.at[block, k],
            recv_sem=recv2.at[block, k],
            device_id={"stn": right, "chan": chan},
            device_id_type=MESH,
        ).wait_recv()

    def own(group):
        @pl.loop(1, nchan)
        def _(step):
            turn(group, step).wait_recv()

        lo, hi = GROUPS[group]
        for k in range(lo, hi):

            @pl.loop(0, RCAP, unroll=4)
            def _(r):
                block = arrived[group][k - lo, source[r]]
                gathered[k, stn, r] = jnp.where(r < count, block, jnp.zeros_like(block))

            push(OWN, k, right, L0)
            push(OWN, k, left, R0)
            push(OWN, k, across, Y0)

    def beside(k):
        if k % 2 == 0:
            arrive(R0, k)
            push(R0, k, left, F0)
            arrive(L0, k)
        else:
            arrive(L0, k)
            push(L0, k, right, F0)
            arrive(R0, k)

    def pair(k):
        arrive(Y0, k)
        push(Y0, k, right, L1)
        push(Y0, k, left, R1)

    def far(k):
        arrive(F0, k)
        push(F0, k, across, F1)

    own(0)
    own(1)
    share(OWN, 0)
    beside(0)
    pair(0)
    own(2)
    own(3)
    beside(1)
    pair(1)
    share(OWN, 1)
    far(0)
    for block in (R0, L0, Y0):
        share(block, 0)
    beside(2)
    beside(3)
    pair(2)
    pair(3)
    far(1)
    for group in range(len(GROUPS)):

        @pl.loop(1, nchan)
        def _(step):
            turn(group, step).wait_send()

    share(R0, 1)
    share(L0, 1)
    share(Y0, 1)
    share(F0, 0)
    early = len(sends)
    far(2)
    far(3)
    share(F0, 1)
    for block in (R1, L1, F1):
        arrive(block, 0)
        arrive(block, 1)
        share(block, 0)
    for copy in sends[:early]:
        copy.wait_send()
    for half in range(2):
        for block in (OWN, R0, L0, Y0):
            from_sibling(block, half)
    for block in (R1, L1):
        arrive(block, 2)
    arrive(R1, 3)
    share(R1, 1)
    arrive(L1, 3)
    share(L1, 1)
    arrive(F1, 2)
    arrive(F1, 3)
    share(F1, 1)
    for half in range(2):
        for block in (F0, R1, L1, F1):
            from_sibling(block, half)
    for copy in sends[early:]:
        copy.wait_send()


def front(volts, taps, survive, owner, stn_count):
    inputs = volts.shape[2]
    lanes = 2 * inputs
    nchan = owner.shape[1]
    dma = pltpu.SemaphoreType.DMA
    return pl.pallas_call(
        front_kernel,
        out_shape=jax.ShapeDtypeStruct((PARTS, stn_count, RCAP, SPAN, lanes), BF16),
        in_specs=[pl.BlockSpec(memory_space=pltpu.HBM)] * 4,
        out_specs=pl.BlockSpec(memory_space=pltpu.VMEM),
        scratch_shapes=[
            pltpu.SMEM(survive.shape, jnp.int32),
            pltpu.SMEM(owner.shape, jnp.int32),
            pltpu.VMEM(taps.shape, F32),
            pltpu.VMEM((2, inputs, NS * FINE), BF16),
            pltpu.VMEM((TAPS * 16, FINE), BF16),
            pltpu.VMEM((NS, TAPS * 16, lanes), F32),
            pltpu.VMEM((KEEP * SPAN, lanes), F32),
            pltpu.VMEM((KEEP, SPAN, lanes), BF16),
            pltpu.VMEM((PARTS, nchan * CAP, SPAN, lanes), BF16),
            *[pltpu.VMEM((hi - lo, nchan * CAP, SPAN, lanes), BF16) for lo, hi in GROUPS],
            pltpu.SMEM((nchan * CAP,), jnp.int32),
            pltpu.SMEM((RCAP,), jnp.int32),
            dma((3,)),
            dma((len(CHUNKS),)),
            dma((len(GROUPS), nchan)),
            dma((len(GROUPS), nchan)),
            dma((8, PARTS)),
            dma((8, PARTS)),
            dma((8, 2)),
            dma((8, 2)),
        ],
        compiler_params=pltpu.CompilerParams(
            collective_id=0, has_side_effects=True, vmem_limit_bytes=48 << 20
        ),
        name="front",
    )(survive, owner, taps, volts)


def correlate_kernel(stn_count, gathered, out_ref, built, sems):
    stn = lax.axis_index("stn")
    low = lax.broadcasted_iota(jnp.int32, (NSPEC, 128), 1) < 64

    def series(n, slot):
        return jnp.concatenate([gathered[k, n, slot].astype(F32) for k in range(PARTS)], 0)

    def store(slot):
        return pltpu.make_async_copy(built.at[slot], out_ref.at[0, slot], sems.at[slot])

    def correlate_slot(slot):
        own = series(stn, slot) * (1.0 / NSPEC)
        turned = swap_halves(own)
        turned = jnp.where(low, turned, -turned)
        left = jnp.concatenate([own, turned], 0).astype(BF16)
        for n in range(0, stn_count, 2):
            first, second = series(n, slot), series(n + 1, slot)
            real = jnp.where(low, first, swap_halves(second))
            imag = jnp.where(low, swap_halves(first), second)
            product = lax.dot_general(
                left,
                jnp.concatenate([real, imag], 0).astype(BF16),
                (((0,), (0,)), ((), ())),
                preferred_element_type=F32,
            )
            built[slot, :, :, n * 64 : (n + 2) * 64] = product.astype(BF16).reshape(2, 64, 128)
        store(slot).start()

    @pl.loop(0, RCAP // SLOTS_STEP)
    def _(step):
        for u in range(SLOTS_STEP):
            correlate_slot(step * SLOTS_STEP + u)

    @pl.loop(0, RCAP)
    def _(slot):
        store(slot).wait()


def correlate(gathered):
    stn_count, lanes = gathered.shape[1], gathered.shape[4]
    inputs = lanes // 2
    return pl.pallas_call(
        functools.partial(correlate_kernel, stn_count),
        out_shape=jax.ShapeDtypeStruct((1, RCAP, 2, inputs, stn_count * inputs), BF16),
        in_specs=[pl.BlockSpec(memory_space=pltpu.VMEM)],
        out_specs=pl.BlockSpec(memory_space=pltpu.HBM),
        scratch_shapes=[
            pltpu.VMEM((RCAP, 2, inputs, stn_count * inputs), BF16),
            pltpu.SemaphoreType.DMA((RCAP,)),
        ],
        compiler_params=pltpu.CompilerParams(vmem_limit_bytes=16 << 20),
        name="correlate",
    )(gathered)


def per_device(volts, taps, survive, owner):
    volts, taps, survive, owner = [pltpu.with_memory_space_constraint(v, pltpu.HBM) for v in (volts, taps, survive.T, owner.T)]
    gathered = front(volts, taps, survive, owner, lax.axis_size("stn"))
    return correlate(gathered)


def solution(mesh):
    return jax.shard_map(
        per_device,
        mesh=mesh,
        in_specs=(P("chan", None, "stn", None), P(), P(), P()),
        out_specs=P("chan", None, None, "stn", None),
        check_vma=False,
    )
```

```python
import functools
import math

import jax
import jax.numpy as jnp
from jax import lax
from jax.experimental import pallas as pl
from jax.experimental.pallas import tpu as pltpu
from jax.sharding import PartitionSpec as P

RCAP = 24
CAP = 2
FINE = 384
TAPS = 16
NSPEC = 32
KEEP = 8
NS = NSPEC + TAPS - 1
F32 = jnp.float32
BF16 = jnp.bfloat16
MESH = pl.DeviceIdType.MESH


def swap_halves(x):
    return pltpu.roll(x, 64, 1)


def trig_tables(chosen, branch):
    product = chosen * branch
    turns = jnp.floor((product + 0.5) * (1.0 / FINE))
    phase = product - turns * FINE
    quarter = jnp.floor((phase + (FINE // 8)) * (4.0 / FINE) + 1e-4)
    angle = (phase - quarter * (FINE // 4)) * (2.0 * math.pi / FINE)
    square = angle * angle
    sine = angle * (
        1.0
        + square
        * (-1.0 / 6 + square * (1.0 / 120 + square * (-1.0 / 5040 + square * (1.0 / 362880))))
    )
    cosine = 1.0 + square * (
        -0.5
        + square
        * (1.0 / 24 + square * (-1.0 / 720 + square * (1.0 / 40320 - square * (1.0 / 3628800))))
    )
    odd = (quarter == 1.0) | (quarter == 3.0)
    c = jnp.where(odd, sine, cosine)
    s = jnp.where(odd, cosine, sine)
    c = jnp.where((quarter == 1.0) | (quarter == 2.0), -c, c)
    s = jnp.where((quarter == 2.0) | (quarter == 3.0), -s, s)
    factor = 1.0 / math.sqrt(FINE)
    return ((c * factor).astype(BF16).astype(F32), (s * factor).astype(BF16).astype(F32))


CHUNKS = ((0, 12), (12, 23), (23, 31), (31, 39), (39, NS))
SLOTS_STEP = 8
PARTS = 4
SPAN = NSPEC // PARTS
GROUPS = ((0, 1), (1, 2), (2, 4))
OWN, Y0, R0, L0, R1, L1, F0, F1 = range(8)
PLACES = {
    OWN: (0, 0), Y0: (0, 1), R0: (1, 0), L0: (3, 0), R1: (1, 1), L1: (3, 1), F0: (2, 0), F1: (2, 1)
}


def front_kernel(
    survive_hbm, owner_hbm, taps_hbm, volts_ref, gathered,
    survive_ref, owner_ref, taps_ref, buf, weights, partial, rows, channels, outbox, arrived0, arrived1, arrived2, pick, source,
    small_sem, load_sem, send1, recv1, send2, recv2, sib_send, sib_recv,
):
    arrived = (arrived0, arrived1, arrived2)
    stn = lax.axis_index("stn")
    chan = lax.axis_index("chan")
    nchan = lax.axis_size("chan")
    x, y, core = stn // 4, (stn // 2) % 2, stn % 2

    def name(dx, dy, dcore=0):
        return ((x + dx) % 4) * 4 + ((y + dy) % 2) * 2 + (core + dcore) % 2

    right, left, across, sibling = name(1, 0), name(3, 0), name(0, 1), name(0, 0, 1)

    def load(n):
        lanes = pl.ds(CHUNKS[n][0] * FINE, (CHUNKS[n][1] - CHUNKS[n][0]) * FINE)
        return pltpu.make_async_copy(
            volts_ref.at[0, :, :, lanes], buf.at[:, :, lanes], load_sem.at[n]
        )

    small = [
        pltpu.make_async_copy(source, target, small_sem.at[n])
        for n, (source, target) in enumerate(
            ((survive_hbm, survive_ref), (taps_hbm, taps_ref), (owner_hbm, owner_ref))
        )
    ]
    for copy in small:
        copy.start()
    for n in range(len(CHUNKS)):
        load(n).start()

    barrier = pltpu.get_barrier_semaphore()
    for other in (right, left, across, sibling):
        pl.semaphore_signal(
            barrier, inc=1, device_id={"stn": other, "chan": chan}, device_id_type=MESH
        )

    @pl.loop(1, nchan)
    def _(step):
        pl.semaphore_signal(
            barrier,
            inc=1,
            device_id={"stn": stn, "chan": (chan + step) % nchan},
            device_id_type=MESH,
        )

    for copy in small:
        copy.wait()

    row = lax.broadcasted_iota(jnp.int32, (KEEP, FINE), 0)
    branch = lax.broadcasted_iota(jnp.int32, (KEEP, FINE), 1).astype(F32)
    chosen = jnp.zeros((KEEP, FINE), jnp.int32)
    for j in range(KEEP):
        chosen = jnp.where(row == j, survive_ref[j, chan], chosen)
    cosine, sine = trig_tables(chosen.astype(F32), branch)
    both = jnp.concatenate([cosine, sine], 0)
    for p in range(TAPS):
        weights[p * 16 : (p + 1) * 16, :] = (both * taps_ref[p : p + 1, :]).astype(BF16)

    targets = []
    owners = [owner_ref[j, chan] for j in range(KEEP)]
    for j in range(KEEP):
        rank = jnp.int32(0)
        for other in range(j):
            rank = rank + (owners[other] == owners[j]).astype(jnp.int32)
        targets.append(owners[j] * CAP + rank)

    for slot in range(nchan * CAP):
        found = jnp.int32(0)
        for j in range(1, KEEP):
            found = jnp.where(targets[j] == slot, j, found)
        pick[slot] = found

    def transform(first, width):
        block = jnp.concatenate(
            [
                buf[:, :, (first + u) * FINE : (first + u + 1) * FINE].reshape(128, FINE)
                for u in range(width)
            ],
            0,
        )
        product = lax.dot_general(
            weights[...], block, (((1,), (1,)), ((), ())), preferred_element_type=F32
        )
        for u in range(width):
            partial[first + u] = product[:, u * 128 : (u + 1) * 128]

    def finish(t):
        total = partial[t, 0:16, :]
        for p in range(1, TAPS):
            total = total + partial[t + p, p * 16 : (p + 1) * 16, :]
        swapped = swap_halves(total[8:16])
        rows[pl.ds(t % SPAN, KEEP, stride=SPAN), :] = total[0:8] + jnp.where(
            lane < 64, swapped, -swapped
        )

    lane = lax.broadcasted_iota(jnp.int32, (KEEP, 128), 1)

    def turn(group, step):
        to = (chan + step) % nchan
        lo, hi = GROUPS[group]
        return pltpu.make_async_remote_copy(
            src_ref=outbox.at[lo:hi, pl.ds(to * CAP, CAP)],
            dst_ref=arrived[group].at[:, pl.ds(chan * CAP, CAP)],
            send_sem=send1.at[group, step],
            recv_sem=recv1.at[group, step],
            device_id={"stn": stn, "chan": to},
            device_id_type=MESH,
        )

    chunk = 0
    done = 0
    for group, (lo, hi) in enumerate(GROUPS):
        for q in range(lo, hi):
            while done < (q + 1) * SPAN:
                load(chunk).wait()
                begin, end = CHUNKS[chunk]
                chunk += 1
                for first in range(begin, end, 2):
                    width = min(2, end - first)
                    transform(first, width)
                    while done + TAPS <= first + width and done < (q + 1) * SPAN:
                        finish(done)
                        done += 1

            for j in range(KEEP):
                channels[j] = rows[j * SPAN : (j + 1) * SPAN, :].astype(BF16)
            for slot in range(nchan * CAP):
                outbox[q, slot] = channels[pick[slot]]

        if group == 0:
            pl.semaphore_wait(barrier, 4 + nchan - 1)

        @pl.loop(0, nchan - 1)
        def _(i):
            turn(group, nchan // 2 + ((i + 1) // 2) * (2 * (i % 2) - 1)).start()

        for q in range(lo, hi):
            mine = pl.ds(chan * CAP, CAP)
            arrived[group][q - lo, mine] = outbox[q, mine]

    counts = []
    count = jnp.int32(0)
    for b in range(nchan):
        for j in range(KEEP):
            count = count + (owner_ref[j, b] == chan).astype(jnp.int32)
        counts.append(count)

    @pl.loop(0, RCAP)
    def _(r):
        skip = jnp.int32(0)
        for b in range(nchan):
            skip = jnp.where(counts[b] <= r, (b + 1) * CAP - counts[b], skip)
        source[r] = jnp.minimum(r + skip, nchan * CAP - 1)

    sends = []

    def part(block, k):
        dx, dy = PLACES[block]
        return gathered.at[k, name(dx, dy)]

    def two(block, half, dcore=0):
        dx, dy = PLACES[block]
        return gathered.at[2 * half : 2 * half + 2, name(dx, dy, dcore)]

    def push(block, k, to, slot):
        copy = pltpu.make_async_remote_copy(
            src_ref=part(block, k),
            dst_ref=part(block, k),
            send_sem=send2.at[slot, k],
            recv_sem=recv2.at[slot, k],
            device_id={"stn": to, "chan": chan},
            device_id_type=MESH,
        )
        copy.start()
        sends.append(copy)

    def share(block, half):
        copy = pltpu.make_async_remote_copy(
            src_ref=two(block, half),
            dst_ref=two(block, half),
            send_sem=sib_send.at[block, half],
            recv_sem=sib_recv.at[block, half],
            device_id={"stn": sibling, "chan": chan},
            device_id_type=MESH,
        )
        copy.start()
        sends.append(copy)

    def from_sibling(block, half):
        pltpu.make_async_remote_copy(
            src_ref=two(block, half, 1),
            dst_ref=two(block, half, 1),
            send_sem=sib_send.at[block, half],
            recv_sem=sib_recv.at[block, half],
            device_id={"stn": sibling, "chan": chan},
            device_id_type=MESH,
        ).wait_recv()

    def arrive(block, k):
        pltpu.make_async_remote_copy(
            src_ref=part(block, k),
            dst_ref=part(block, k),
            send_sem=send2.at[block, k],
            recv_sem=recv2.at[block, k],
            device_id={"stn": right, "chan": chan},
            device_id_type=MESH,
        ).wait_recv()

    def own(group):
        @pl.loop(1, nchan)
        def _(step):
            turn(group, step).wait_recv()

        lo, hi = GROUPS[group]
        for k in range(lo, hi):

            @pl.loop(0, RCAP, unroll=4)
            def _(r):
                block = arrived[group][k - lo, source[r]]
                gathered[k, stn, r] = jnp.where(r < count, block, jnp.zeros_like(block))

            push(OWN, k, right, L0)
            push(OWN, k, left, R0)
            push(OWN, k, across, Y0)

    def beside(k):
        if k % 2 == 0:
            arrive(R0, k)
            push(R0, k, left, F0)
            arrive(L0, k)
        else:
            arrive(L0, k)
            push(L0, k, right, F0)
            arrive(R0, k)

    def pair(k):
        arrive(Y0, k)
        push(Y0, k, right, L1)
        push(Y0, k, left, R1)

    def far(k):
        arrive(F0, k)
        push(F0, k, across, F1)

    own(0)
    own(1)
    share(OWN, 0)
    beside(0)
    pair(0)
    own(2)
    beside(1)
    pair(1)
    share(OWN, 1)
    far(0)
    for block in (R0, L0, Y0):
        share(block, 0)
    beside(2)
    beside(3)
    pair(2)
    pair(3)
    far(1)
    for group in range(len(GROUPS)):

        @pl.loop(1, nchan)
        def _(step):
            turn(group, step).wait_send()

    share(R0, 1)
    share(L0, 1)
    share(Y0, 1)
    share(F0, 0)
    early = len(sends)
    far(2)
    far(3)
    share(F0, 1)
    for block in (R1, L1, F1):
        arrive(block, 0)
        arrive(block, 1)
        share(block, 0)
    for copy in sends[:early]:
        copy.wait_send()
    for half in range(2):
        for block in (OWN, R0, L0, Y0):
            from_sibling(block, half)
    for block in (R1, L1):
        arrive(block, 2)
    arrive(R1, 3)
    share(R1, 1)
    arrive(L1, 3)
    share(L1, 1)
    arrive(F1, 2)
    arrive(F1, 3)
    share(F1, 1)
    for half in range(2):
        for block in (F0, R1, L1, F1):
            from_sibling(block, half)
    for copy in sends[early:]:
        copy.wait_send()


def front(volts, taps, survive, owner, stn_count):
    inputs = volts.shape[2]
    lanes = 2 * inputs
    nchan = owner.shape[1]
    dma = pltpu.SemaphoreType.DMA
    return pl.pallas_call(
        front_kernel,
        out_shape=jax.ShapeDtypeStruct((PARTS, stn_count, RCAP, SPAN, lanes), BF16),
        in_specs=[pl.BlockSpec(memory_space=pltpu.HBM)] * 4,
        out_specs=pl.BlockSpec(memory_space=pltpu.VMEM),
        scratch_shapes=[
            pltpu.SMEM(survive.shape, jnp.int32),
            pltpu.SMEM(owner.shape, jnp.int32),
            pltpu.VMEM(taps.shape, F32),
            pltpu.VMEM((2, inputs, NS * FINE), BF16),
            pltpu.VMEM((TAPS * 16, FINE), BF16),
            pltpu.VMEM((NS, TAPS * 16, lanes), F32),
            pltpu.VMEM((KEEP * SPAN, lanes), F32),
            pltpu.VMEM((KEEP, SPAN, lanes), BF16),
            pltpu.VMEM((PARTS, nchan * CAP, SPAN, lanes), BF16),
            *[pltpu.VMEM((hi - lo, nchan * CAP, SPAN, lanes), BF16) for lo, hi in GROUPS],
            pltpu.SMEM((nchan * CAP,), jnp.int32),
            pltpu.SMEM((RCAP,), jnp.int32),
            dma((3,)),
            dma((len(CHUNKS),)),
            dma((len(GROUPS), nchan)),
            dma((len(GROUPS), nchan)),
            dma((8, PARTS)),
            dma((8, PARTS)),
            dma((8, 2)),
            dma((8, 2)),
        ],
        compiler_params=pltpu.CompilerParams(
            collective_id=0, has_side_effects=True, vmem_limit_bytes=48 << 20
        ),
        name="front",
    )(survive, owner, taps, volts)


def correlate_kernel(stn_count, gathered, out_ref, built, sems):
    stn = lax.axis_index("stn")
    low = lax.broadcasted_iota(jnp.int32, (NSPEC, 128), 1) < 64

    def series(n, slot):
        return jnp.concatenate([gathered[k, n, slot].astype(F32) for k in range(PARTS)], 0)

    def store(slot):
        return pltpu.make_async_copy(built.at[slot], out_ref.at[0, slot], sems.at[slot])

    def correlate_slot(slot):
        own = series(stn, slot) * (1.0 / NSPEC)
        turned = swap_halves(own)
        turned = jnp.where(low, turned, -turned)
        left = jnp.concatenate([own, turned], 0).astype(BF16)
        for n in range(0, stn_count, 2):
            first, second = series(n, slot), series(n + 1, slot)
            real = jnp.where(low, first, swap_halves(second))
            imag = jnp.where(low, swap_halves(first), second)
            product = lax.dot_general(
                left,
                jnp.concatenate([real, imag], 0).astype(BF16),
                (((0,), (0,)), ((), ())),
                preferred_element_type=F32,
            )
            built[slot, :, :, n * 64 : (n + 2) * 64] = product.astype(BF16).reshape(2, 64, 128)
        store(slot).start()

    @pl.loop(0, RCAP // SLOTS_STEP)
    def _(step):
        for u in range(SLOTS_STEP):
            correlate_slot(step * SLOTS_STEP + u)

    @pl.loop(0, RCAP)
    def _(slot):
        store(slot).wait()


def correlate(gathered):
    stn_count, lanes = gathered.shape[1], gathered.shape[4]
    inputs = lanes // 2
    return pl.pallas_call(
        functools.partial(correlate_kernel, stn_count),
        out_shape=jax.ShapeDtypeStruct((1, RCAP, 2, inputs, stn_count * inputs), BF16),
        in_specs=[pl.BlockSpec(memory_space=pltpu.VMEM)],
        out_specs=pl.BlockSpec(memory_space=pltpu.HBM),
        scratch_shapes=[
            pltpu.VMEM((RCAP, 2, inputs, stn_count * inputs), BF16),
            pltpu.SemaphoreType.DMA((RCAP,)),
        ],
        compiler_params=pltpu.CompilerParams(vmem_limit_bytes=16 << 20),
        name="correlate",
    )(gathered)


def per_device(volts, taps, survive, owner):
    volts, taps, survive, owner = [pltpu.with_memory_space_constraint(v, pltpu.HBM) for v in (volts, taps, survive.T, owner.T)]
    gathered = front(volts, taps, survive, owner, lax.axis_size("stn"))
    return correlate(gathered)


def solution(mesh):
    return jax.shard_map(
        per_device,
        mesh=mesh,
        in_specs=(P("chan", None, "stn", None), P(), P(), P()),
        out_specs=P("chan", None, None, "stn", None),
        check_vma=False,
    )
```
